32 devices in a mesh: group: 2 (over y), member: 16 (over z, x, core).
Axes of the slice: x: 2, y: 2, z: 4, core: 2. Of those that a mesh axis runs over, the one named last changes fastest.
Arguments:
- rows: float32 [16384, 1024], P(('group', 'member'))
- old_list: int32 [16384], P(('group', 'member')), may hold values from 0 to 63
- old_centroids: float32 [64, 1024], replicated, may hold values from -6 to 6
- dest_device: int32 [16384, 1], P(('group', 'member')), may hold values from 0 to 31; in each aligned block of 512 rows (0 to 511, 512 to 1023, ...) at most 32 rows name the same one
- new_local: int32 [16384], P(('group', 'member')), may hold values from 0 to 1
- centroids: float32 [4, 1024], P('group'), may hold values from -6 to 6
Outputs:
- whitened: float32 [32768, 1024], P(('group', 'member'))
- factors: float32 [4, 1024, 1024], P('group')
The draws below stay inside these ranges and needn't reach their ends.
Inputs may be any that keep to these rules, and one draw needn't show every extreme that they name: `dest_device`: among the rows of one device, no destination is named by more than 32 rows, a bound that some block reaches.
All inputs are finite; a program needn't handle non-finite values.
Results may differ from the reference program's by a relative error of at most 0.0003.
Values sent between devices are 32-bit elements; how exact they have to be, the bound alone decides.
No kernel may reach another device: no remote copies, remote signals or barrier semaphores. Data moves between devices by JAX's collectives and lax.ppermute only.
A program may use at most 128 MiB of HBM per device.

```python
import math
import jax
import jax.numpy as jnp
import numpy as np
from jax import lax

D = 1024
ROW_DEV = 512
LIST_GRP = 2
OLD = 64
CAP = 32
ROWS = 16384
LISTS = 4
N_GROUP = 2
N_MEMBER = 16
DEVICES = 32


def draw_rows(key, part):
    first, second = jax.random.split(key)
    base = jax.random.normal(first, (ROWS, D), jnp.float32)
    scales = jnp.exp(jax.random.uniform(second, (D,), jnp.float32, 0.0, 1.4))
    mixed = base + 0.8 * jnp.roll(base, 1, axis=1)
    return (mixed * scales[None, :]).astype(jnp.float32)


def with_ends(entries, rng, smallest, largest):
    place = [jax.random.randint(jax.random.fold_in(rng, axis), (), 0, length) for axis, length in enumerate(entries.shape)]
    main_axis = entries.shape.index(max(entries.shape))
    neighbour = place[:main_axis] + [(place[main_axis] + 1) % entries.shape[main_axis]] + place[main_axis + 1:]
    return entries.at[tuple(place)].set(smallest).at[tuple(neighbour)].set(largest)


def levels(own_key, extent, pieces, smallest, largest):
    def one(dim, blocks):
        draws = jax.random.uniform(jax.random.fold_in(jax.random.fold_in(own_key, 6), dim), (blocks,), jnp.float32, smallest / len(pieces), largest / len(pieces))
        return jnp.repeat(jnp.exp(draws), extent[dim] // blocks).reshape((-1,) + (1,) * (len(extent) - dim - 1))

    gain = one(*pieces[0])
    for cut in pieces[1:]:
        gain = gain * one(*cut)
    return gain


def deal_out(key, own, number, rows, count, top, limit, skew):
    ranking = jax.random.permutation(key, count)
    heavy_load, ordinary = load_shares(count, rows * top, limit, skew, True), load_shares(count, rows * top, limit, skew, False)
    places = jnp.arange(count)

    def named(tallies, rotation):
        used = int((tallies > 0).sum())
        fixed = max(1, used // 4)
        moved = fixed + (places - fixed + rotation * (used - fixed)) % max(1, count - fixed)
        return jnp.zeros((count,), jnp.int32).at[ranking[jnp.where(places < fixed, places, moved)]].set(jnp.asarray(tallies, jnp.int32))

    tallies = jnp.where(number % 4 == 0, named(heavy_load, number // 4), named(ordinary, number - number // 4 - 1))
    mixed = jax.random.permutation(jax.random.fold_in(own, 3), count)
    donor, sink = mixed[0:count // 2 * 2:2], mixed[1:count // 2 * 2:2]
    slack = jnp.minimum(tallies[donor] - 1, limit - tallies[sink]) // 2
    slack = jnp.where((donor == ranking[0]) | (sink == ranking[0]) | (tallies[sink] == 0), 0, jnp.maximum(slack, 0))
    moved = jax.random.randint(jax.random.fold_in(own, 4), (count // 2,), 0, 1 << 20) % (slack + 1)
    tallies = tallies.at[donor].add(-moved).at[sink].add(moved)
    items = jnp.searchsorted(jnp.cumsum(tallies), jnp.arange(rows * top), side="right").astype(jnp.int32)
    grid = items.reshape(top, rows).T
    grid = grid[jax.random.permutation(jax.random.fold_in(own, 1), rows)]
    rotation = jax.random.randint(jax.random.fold_in(own, 2), (rows, 1), 0, top)
    return jnp.take_along_axis(grid, (jnp.arange(top)[None, :] + rotation) % top, axis=1)


def load_shares(amount, total, limit, lean, full):
    loads = [(1 << 20) // math.isqrt(rank ** lean) + 1 for rank in range(1, amount + 1)]
    largest = limit if full else min(limit, max(-(-total // amount), total * loads[0] // sum(loads)))
    least = 1 if total - largest >= amount - 1 else 0
    given, surplus = [largest] + [least] * (amount - 1), total - largest - least * (amount - 1)
    while surplus > 0:
        free = [i for i in range(1, amount) if given[i] < largest] or [i for i in range(1, amount) if given[i] < limit]
        pool, budget = sum([loads[i] for i in free]), surplus
        for i in free:
            extra = min(limit - given[i], max(1, budget * loads[i] // pool), surplus)
            given[i] = given[i] + extra
            surplus = surplus - extra
    return np.array(given)


def normal_values(key, shape, width, bound, pieces=(), kind=jnp.bfloat16):
    drawn = width * jax.random.normal(key, shape, jnp.float32)
    if pieces:
        drawn = drawn * levels(key, shape, pieces, -0.22, 0.18)
    return jnp.clip(drawn, -bound, bound).astype(kind)


def setup_inputs(seed: int = 0) -> dict:
    splits = jax.random.split(jax.random.key(seed), 7)
    rows = draw_rows(jax.random.fold_in(splits[6], 71), 0)
    old_list = with_ends(jax.random.randint(splits[1], (ROWS,), 0, OLD), jax.random.fold_in(splits[1], 1), 0, OLD - 1).astype(jnp.int32)
    old_centroids = normal_values(splits[2], (OLD, D), 1.0, 6.0, (), jnp.float32)
    dest_device_keys = jax.random.split(jax.random.fold_in(splits[3], 1), ROWS // ROW_DEV)
    dest_device_turns = jax.random.permutation(jax.random.fold_in(splits[3], 3), ROWS // ROW_DEV)
    dest_device = jax.vmap(lambda own, number: deal_out(jax.random.fold_in(splits[3], 2), own, number, ROW_DEV, DEVICES, 1, CAP, 2))(dest_device_keys, dest_device_turns).reshape((ROWS, 1))
    new_local = with_ends(jax.random.randint(splits[4], (ROWS,), 0, LIST_GRP), jax.random.fold_in(splits[4], 1), 0, LIST_GRP - 1).astype(jnp.int32)
    centroids = normal_values(splits[5], (LISTS, D), 1.0, 6.0, ((0, 2),), jnp.float32)
    return dict(rows=rows, old_list=old_list, old_centroids=old_centroids, dest_device=dest_device, new_local=new_local, centroids=centroids)


ridge = 0.1

def reference(rows, old_list, old_centroids, dest_device, new_local, centroids):
    devices = N_GROUP * N_MEMBER
    vectors = rows + old_centroids[old_list]
    dest = dest_device[:, 0].astype(jnp.int32)
    source = (jnp.arange(ROWS) // ROW_DEV).astype(jnp.int32)
    blocks = dest.reshape(devices, ROW_DEV)
    onehot = (blocks[:, :, None] == jnp.arange(devices, dtype=jnp.int32)[None, None, :]).astype(jnp.int32)
    ranks = jnp.sum(jnp.cumsum(onehot, axis=1) * onehot, axis=2) - 1
    position = (dest * devices * CAP + source * CAP + ranks.reshape(-1)).astype(jnp.int32)
    slots = devices * devices * CAP
    tag_all = jnp.zeros((slots,), jnp.int32).at[position].set(new_local.astype(jnp.int32) + 1)
    buffer = jnp.zeros((slots, D), jnp.float32).at[position].set(vectors)
    buffer = buffer.reshape(N_GROUP, N_MEMBER * devices * CAP, D)
    tag_all = tag_all.reshape(N_GROUP, N_MEMBER * devices * CAP)
    cents = centroids.reshape(N_GROUP, LIST_GRP, D)

    def per_group(items):
        block, tags, cent = items
        select = (tags[:, None] == jnp.arange(1, LIST_GRP + 1, dtype=jnp.int32)[None, :]).astype(jnp.float32)
        residual = jnp.where(tags[:, None] > 0, block - jnp.dot(select, cent, precision=lax.Precision.HIGHEST), 0.0)
        counts = jnp.sum(select, axis=0)
        result = jnp.zeros_like(residual)
        chol = []
        for j in range(LIST_GRP):
            masked = residual * select[:, j:j + 1]
            gram = lax.dot_general(masked, masked, (((0,), (0,)), ((), ())), precision=lax.Precision.HIGHEST)
            cov = gram / jnp.maximum(counts[j], 1.0) + ridge * jnp.eye(D, dtype=jnp.float32)
            lower = jnp.linalg.cholesky(cov)
            chol.append(lower)
            solved = jax.scipy.linalg.solve_triangular(lower, residual.T, lower=True).T
            result = result + select[:, j:j + 1] * solved
        return (jnp.stack(chol), result)
    lowers, outs = lax.map(per_group, (buffer, tag_all, cents))
    return (outs.reshape(slots, D), lowers.reshape(LISTS, D, D))
```

```python
import jax
import jax.numpy as jnp
from jax import lax
from jax.experimental import pallas as pl
from jax.experimental.pallas import tpu as pltpu
from jax.sharding import PartitionSpec as P

ridge = 0.1
f32 = jnp.float32
bf16 = jnp.bfloat16
BL = 128
SUB = 8


def split(x):
    hi = x.astype(bf16)
    return hi, (x - hi.astype(f32)).astype(bf16)


def dot_nt(a, b):
    return lax.dot_general(a, b, (((1,), (1,)), ((), ())), preferred_element_type=f32)


def dot_nn(a, b):
    return lax.dot_general(a, b, (((1,), (0,)), ((), ())), preferred_element_type=f32)


def blocks(n):
    nb = n // BL
    return [(i, j) for j in range(nb) for i in range(j, nb)]


def gram_body(rel, res_ref, code_ref, out_ref, th_ref, tl_ref, h_ref, l_ref):
    g = pl.program_id(0)
    rows, n = res_ref.shape

    @pl.when(g == 0)
    def _():
        for j in range(0, n, BL):
            x = res_ref[:, j : j + BL]
            hi, lo = split(x)
            h_ref[:, j : j + BL] = hi
            l_ref[:, j : j + BL] = lo
            xt = x.T
            hi, lo = split(xt)
            th_ref[j : j + BL, :] = hi
            tl_ref[j : j + BL, :] = lo

    mask = code_ref[...] == 2 * g + rel
    place = {b: p for p, b in enumerate(blocks(n))}
    for j in range(0, n, 2 * BL):
        mh = jnp.where(mask, h_ref[:, j : j + 2 * BL], jnp.zeros((), bf16))
        ml = jnp.where(mask, l_ref[:, j : j + 2 * BL], jnp.zeros((), bf16))
        th = th_ref[j:n, :]
        tl = tl_ref[j:n, :]
        prod = dot_nn(th, mh) + (dot_nn(th, ml) + dot_nn(tl, mh))
        for i in range(j, n, BL):
            for c in (j, j + BL):
                if i >= c:
                    p = place[(i // BL, c // BL)]
                    out_ref[0, p * BL : (p + 1) * BL, :] = prod[i - j : i - j + BL, c - j : c - j + BL]


def gram(res, code, n_group, rel):
    rows, n = res.shape
    size = len(blocks(n)) * BL
    return pl.pallas_call(
        lambda *refs: gram_body(rel, *refs),
        grid=(n_group,),
        in_specs=[
            pl.BlockSpec((rows, n), lambda g: (0, 0)),
            pl.BlockSpec((rows, 1), lambda g: (0, 0)),
        ],
        out_specs=pl.BlockSpec((1, size, BL), lambda g: (g, 0, 0)),
        out_shape=jax.ShapeDtypeStruct((n_group, size, BL), f32),
        scratch_shapes=[
            pltpu.VMEM((n, rows), bf16),
            pltpu.VMEM((n, rows), bf16),
            pltpu.VMEM((rows, n), bf16),
            pltpu.VMEM((rows, n), bf16),
        ],
        compiler_params=pltpu.CompilerParams(vmem_limit_bytes=40 << 20),
        cost_estimate=pl.CostEstimate(
            flops=3 * n_group * rows * n * n, bytes_accessed=4 * (rows * n + n_group * size * BL), transcendentals=0
        ),
        name="gram",
    )(res, code)


def diag_group(b, tt, s):
    lane = lax.broadcasted_iota(jnp.int32, (SUB, BL), 1)
    sub = lax.broadcasted_iota(jnp.int32, (SUB, BL), 0)
    base = SUB * s
    rows = [jnp.broadcast_to(b[base + t : base + t + 1, :], (SUB, BL)) for t in range(SUB)]
    schur = {}
    for i in range(SUB):
        for u in range(i + 1):
            schur[i, u] = jnp.broadcast_to(rows[i][:, base + u : base + u + 1], (SUB, BL))
    panel = (lane >= base) & (lane < base + SUB)
    fwd = [jnp.where(panel, jnp.where(lane == base + t, 1.0, 0.0), rows[t]) for t in range(SUB)]
    pivot, inv, mult = [], [], {}
    for t in range(SUB):
        pivot.append(schur[t, t])
        inv.append(1.0 / schur[t, t])
        for i in range(t + 1, SUB):
            mult[i, t] = schur[i, t] * inv[t]
        for u in range(t + 1, SUB):
            for i in range(u, SUB):
                schur[i, u] = schur[i, u] - mult[u, t] * schur[i, t]
        for i in range(t + 1, SUB):
            fwd[i] = fwd[i] - mult[i, t] * fwd[t]
    back = [None] * SUB
    for t in reversed(range(SUB)):
        w = fwd[t] * inv[t]
        for i in range(SUB - 1, t, -1):
            w = w - mult[i, t] * back[i]
        back[t] = w
    for g in range(s + 1, BL // SUB):
        x = b[SUB * g : SUB * g + SUB, :]
        even, odd = 0.0, 0.0
        for u in range(0, SUB, 2):
            even = even + jnp.broadcast_to(x[:, base + u : base + u + 1], (SUB, BL)) * back[u]
            odd = odd + jnp.broadcast_to(x[:, base + u + 1 : base + u + 2], (SUB, BL)) * back[u + 1]
        b[SUB * g : SUB * g + SUB, :] = jnp.where(panel, 0.0, x) - (even + odd)
    out = jnp.zeros((SUB, BL), f32)
    for t in range(SUB):
        row = jnp.where(lane <= base + t, fwd[t] * lax.rsqrt(pivot[t]), 0.0)
        out = jnp.where(sub == t, row, out)
    tt[base : base + SUB, :] = out


def chol_body(n, scale_ref, pa_ref, pb_ref, out_ref, w_ref, b_ref, t_ref, h1_ref, h2_ref):
    nb = n // BL
    order = blocks(n)
    place = {b: p for p, b in enumerate(order)}
    half = len(order) // 2
    scale = scale_ref[0]
    row = lax.broadcasted_iota(jnp.int32, (BL, BL), 0)
    col = lax.broadcasted_iota(jnp.int32, (BL, BL), 1)
    for p, (i, j) in enumerate(order):
        src, q = (pa_ref, p) if p < half else (pb_ref, p - half)
        x = src[q * BL : (q + 1) * BL, :] * scale
        if i == j:
            x = x + jnp.where(row == col, ridge, 0.0)
        w_ref[i * BL : (i + 1) * BL, j * BL : (j + 1) * BL] = x

    @pl.loop(0, nb)
    def _(k):
        o = pl.multiple_of(k * BL, BL)
        b_ref[...] = w_ref[pl.ds(o, BL), pl.ds(o, BL)]
        for s in range(BL // SUB):
            diag_group(b_ref, t_ref, s)
        out_ref[pl.ds(pl.multiple_of((len(order) + k) * BL, BL), BL), :] = t_ref[...]
        for kk in range(nb):

            @pl.when(k == kk)
            def _():
                c = kk * BL
                th, tl = split(t_ref[...])
                tcat = jnp.concatenate([th, tl, th, tl], axis=1)
                for i in range(c, n, BL):
                    ah, al = split(w_ref[i : i + BL, c : c + BL])
                    x = dot_nt(jnp.concatenate([ah, ah, al, al], axis=1), tcat)
                    if i == c:
                        x = jnp.where(row >= col, x, 0.0)
                    p = place[(i // BL, kk)]
                    out_ref[p * BL : (p + 1) * BL, :] = x
                    if i > c:
                        xh, xl = split(x)
                        h1_ref[i : i + BL, :] = jnp.concatenate([xh, xh, xl, xl], axis=1)
                        h2_ref[i : i + BL, :] = jnp.concatenate([xh, xl, xh, xl], axis=1)
                j = c + BL
                while j < n:
                    wide = BL if (j // BL) % 2 == 1 else 2 * BL
                    w_ref[j:n, j : j + wide] = w_ref[j:n, j : j + wide] - dot_nt(
                        h1_ref[j:n, :], h2_ref[j : j + wide, :]
                    )
                    j += wide


def chol(pa, pb, scale, n):
    nb = n // BL
    size = len(blocks(n)) * BL
    return pl.pallas_call(
        lambda *refs: chol_body(n, *refs),
        in_specs=[
            pl.BlockSpec(memory_space=pltpu.SMEM),
            pl.BlockSpec(memory_space=pltpu.VMEM),
            pl.BlockSpec(memory_space=pltpu.VMEM),
        ],
        out_specs=pl.BlockSpec(memory_space=pltpu.VMEM),
        out_shape=jax.ShapeDtypeStruct((size + n, BL), f32),
        scratch_shapes=[
            pltpu.VMEM((n, n), f32),
            pltpu.VMEM((BL, BL), f32),
            pltpu.VMEM((BL, BL), f32),
            pltpu.VMEM((n, 4 * BL), bf16),
            pltpu.VMEM((n, 4 * BL), bf16),
        ],
        compiler_params=pltpu.CompilerParams(vmem_limit_bytes=40 << 20),
        cost_estimate=pl.CostEstimate(flops=40 * n * n * n, bytes_accessed=8 * size * BL, transcendentals=0),
        name="chol",
    )(scale, pa, pb)


def whiten_body(n, mine_ref, res_ref, tag_ref, own_ref, other_ref, out_ref, fac_ref, lh_ref, ll_ref, th_ref, tl_ref, wh_ref, wl_ref):
    step = pl.program_id(0)
    order = blocks(n)
    nb = n // BL
    mine = mine_ref[0]

    @pl.when(step == 0)
    def _():
        for src, slot, dst in ((own_ref, 0, mine), (other_ref, 1, 1 - mine)):
            fac_ref[dst] = jnp.zeros((n, n), f32)
            for p, (i, j) in enumerate(order):
                x = src[p * BL : (p + 1) * BL, :]
                fac_ref[dst, i * BL : (i + 1) * BL, j * BL : (j + 1) * BL] = x
                hi, lo = split(x)
                lh_ref[slot, i * BL : (i + 1) * BL, j * BL : (j + 1) * BL] = hi
                ll_ref[slot, i * BL : (i + 1) * BL, j * BL : (j + 1) * BL] = lo
            hi, lo = split(src[len(order) * BL :, :])
            th_ref[slot] = hi
            tl_ref[slot] = lo

    tag = tag_ref[...]
    for slot in range(2):
        which = mine if slot == 0 else 1 - mine
        mask = tag == which + 1
        for k in range(nb):
            c = k * BL
            acc = jnp.where(mask, res_ref[:, c : c + BL], 0.0)
            if k:
                lh = lh_ref[slot, c : c + BL, :c]
                ll = ll_ref[slot, c : c + BL, :c]
                wh = wh_ref[:, :c]
                wl = wl_ref[:, :c]
                acc = acc - (dot_nt(wh, lh) + (dot_nt(wh, ll) + dot_nt(wl, lh)))
            ah, al = split(acc)
            th = th_ref[slot, c : c + BL, :]
            tl = tl_ref[slot, c : c + BL, :]
            x = dot_nt(ah, th) + (dot_nt(ah, tl) + dot_nt(al, th))
            hi, lo = split(x)
            wh_ref[:, c : c + BL] = hi
            wl_ref[:, c : c + BL] = lo
            if slot == 0:
                out_ref[:, c : c + BL] = x
            else:
                out_ref[:, c : c + BL] = jnp.where(mask, x, out_ref[:, c : c + BL])


def whiten(res, tags, own, other, mine, tile):
    rows, n = res.shape
    size = own.shape[0]
    whole = lambda s: (0, 0)
    return pl.pallas_call(
        lambda *refs: whiten_body(n, *refs),
        grid=(rows // tile,),
        in_specs=[
            pl.BlockSpec(memory_space=pltpu.SMEM),
            pl.BlockSpec((tile, n), lambda s: (s, 0)),
            pl.BlockSpec((tile, 1), lambda s: (s, 0)),
            pl.BlockSpec((size, BL), whole),
            pl.BlockSpec((size, BL), whole),
        ],
        out_specs=[
            pl.BlockSpec((tile, n), lambda s: (s, 0)),
            pl.BlockSpec((2, n, n), lambda s: (0, 0, 0)),
        ],
        out_shape=[jax.ShapeDtypeStruct((rows, n), f32), jax.ShapeDtypeStruct((2, n, n), f32)],
        scratch_shapes=[
            pltpu.VMEM((2, n, n), bf16),
            pltpu.VMEM((2, n, n), bf16),
            pltpu.VMEM((2, n, BL), bf16),
            pltpu.VMEM((2, n, BL), bf16),
            pltpu.VMEM((tile, n), bf16),
            pltpu.VMEM((tile, n), bf16),
        ],
        compiler_params=pltpu.CompilerParams(vmem_limit_bytes=56 << 20),
        cost_estimate=pl.CostEstimate(flops=12 * rows * n * n, bytes_accessed=16 * n * n, transcendentals=0),
        name="whiten",
    )(mine, res, tags, own, other)


def flip(x, axis, bit):
    size = lax.axis_size(axis)
    return lax.ppermute(x, axis, [(i, i ^ (1 << bit)) for i in range(size)])


def bit_of(axis, bit):
    return (lax.axis_index(axis) >> bit) & 1


def halve(x, axis, bit, dim):
    b = bit_of(axis, bit)
    got = flip(lax.dynamic_slice_in_dim(x, 1 - b, 1, dim), axis, bit)
    return lax.dynamic_slice_in_dim(x, b, 1, dim) + got


def double(x, axis, bit, dim):
    got = flip(x, axis, bit)
    low = bit_of(axis, bit) == 0
    return jnp.where(low, jnp.concatenate([x, got], dim), jnp.concatenate([got, x], dim))


def sum_and_share(part, n_group, n_member):
    gbits = n_group.bit_length() - 1
    mbits = n_member.bit_length() - 1
    rows = part.shape[1]
    shape = (2,) * gbits + (2,) * (mbits - 1)
    ghalf = [("group", b, gbits - 1 - b) for b in range(gbits)]
    mhalf = [("member", b, gbits + b - 1) for b in range(1, mbits)]
    plans = [ghalf + mhalf, mhalf[:1] + ghalf + mhalf[1:]]
    gathers = [mhalf[::-1], mhalf[:1] + mhalf[:0:-1]]
    parts = [
        part[:, c * (rows // 2) : (c + 1) * (rows // 2)].reshape(shape + (rows >> mbits, BL)) for c in range(2)
    ]
    for step in range(gbits + mbits - 1):
        parts = [halve(parts[c], *plans[c][step]) for c in range(2)]
    for step in range(mbits - 1):
        parts = [double(parts[c], *gathers[c][step]) for c in range(2)]
    return [p.reshape(rows // 2, BL) for p in parts]


def on_device(rows, old_list, old_centroids, dest_device, new_local, centroids):
    n_group = lax.axis_size("group")
    n_member = lax.axis_size("member")
    devices = n_group * n_member
    row_dev, width = rows.shape
    lists = centroids.shape[0]
    capacity = max(2, 2 * row_dev // devices)
    group = lax.axis_index("group")
    core = lax.axis_index("member") & 1

    every = jnp.zeros((n_group,) + centroids.shape, f32)
    for shift in range(n_group):
        got = centroids
        if shift:
            got = lax.ppermute(centroids, "group", [(i, (i + shift) % n_group) for i in range(n_group)])
        every = lax.dynamic_update_index_in_dim(every, got, (group - shift) % n_group, 0)
    every = every.reshape(n_group * lists, width)

    dest = dest_device[:, 0]
    new_list = (dest // n_member) * lists + new_local
    old_hot = (old_list[:, None] == jnp.arange(old_centroids.shape[0], dtype=jnp.int32)[None, :]).astype(f32)
    new_hot = (new_list[:, None] == jnp.arange(n_group * lists, dtype=jnp.int32)[None, :]).astype(f32)
    vectors = rows + jnp.dot(old_hot, old_centroids, precision=lax.Precision.HIGHEST)
    residual = vectors - jnp.dot(new_hot, every, precision=lax.Precision.HIGHEST)

    onehot = (dest[:, None] == jnp.arange(devices, dtype=jnp.int32)[None, :]).astype(jnp.int32)
    ranks = jnp.sum(jnp.cumsum(onehot, axis=0) * onehot, axis=1) - 1
    position = dest * capacity + ranks
    outgoing = jnp.zeros((devices * capacity, width), f32).at[position].set(residual)
    out_tags = jnp.zeros((devices * capacity,), jnp.int32).at[position].set(new_local + 1)
    sent = jnp.sum(new_hot, axis=0).astype(jnp.int32).reshape(n_group, lists)
    info = jnp.concatenate(
        [out_tags.reshape(devices, capacity), jnp.repeat(sent, n_member, axis=0)], axis=1
    )
    axes = ("group", "member")
    info = lax.all_to_all(info.reshape(devices, 1, -1), axes, split_axis=0, concat_axis=0, tiled=True)[:, 0]
    arrived = lax.all_to_all(
        outgoing.reshape(devices, capacity, width), axes, split_axis=0, concat_axis=0, tiled=True
    ).reshape(devices * capacity, width)
    tags = info[:, :capacity].reshape(-1, 1)
    counts = jnp.sum(info[:, capacity:], axis=0).astype(f32)

    code = ((dest // n_member) * 2 + (new_local ^ core))[:, None]
    away = gram(residual, code, n_group, 1)
    part = gram(residual, code, n_group, 0) + flip(away, "member", 0)
    pa, pb = sum_and_share(part, n_group, n_member)
    count = lax.dynamic_index_in_dim(counts, core, 0, keepdims=True)
    own = chol(pa, pb, 1.0 / jnp.maximum(count, 1.0), width)
    other = flip(own, "member", 0)
    result, factors = whiten(arrived, tags, own, other, core.reshape(1), min(256, devices * capacity))
    return (result, factors)


def solution(mesh):
    return jax.shard_map(
        on_device,
        mesh=mesh,
        in_specs=(
            P(("group", "member"), None),
            P(("group", "member")),
            P(),
            P(("group", "member"), None),
            P(("group", "member")),
            P("group", None),
        ),
        out_specs=(P(("group", "member"), None), P("group", None, None)),
        check_vma=False,
    )
```

```python
import jax
import jax.numpy as jnp
from jax import lax
from jax.experimental import pallas as pl
from jax.experimental.pallas import tpu as pltpu
from jax.sharding import PartitionSpec as P


ridge = 0.1
f32 = jnp.float32
bf16 = jnp.bfloat16
BL = 128
SUB = 8


def split(x):
    hi = x.astype(bf16)
    return hi, (x - hi.astype(f32)).astype(bf16)


def dot_nt(a, b):
    return lax.dot_general(a, b, (((1,), (1,)), ((), ())), preferred_element_type=f32)


def dot_nn(a, b):
    return lax.dot_general(a, b, (((1,), (0,)), ((), ())), preferred_element_type=f32)


def dot3(a, b):
    ah, al = split(a)
    bh, bl = split(b)
    return dot_nn(ah, bh) + (dot_nn(ah, bl) + dot_nn(al, bh))


def blocks(n):
    nb = n // BL
    return [(i, j) for j in range(nb) for i in range(j, nb)]


def gram_body(rel, res_ref, code_ref, out_ref, th_ref, tl_ref, h_ref, l_ref):
    g = pl.program_id(0)
    _, n = res_ref.shape

    @pl.when(g == 0)
    def _():
        for j in range(0, n, BL):
            x = res_ref[:, j : j + BL]
            hi, lo = split(x)
            h_ref[:, j : j + BL] = hi
            l_ref[:, j : j + BL] = lo
            xt = x.T
            hi, lo = split(xt)
            th_ref[j : j + BL, :] = hi
            tl_ref[j : j + BL, :] = lo

    mask = code_ref[...] == 2 * g + rel
    place = {b: p for p, b in enumerate(blocks(n))}
    for j in range(0, n, 2 * BL):
        mh = jnp.where(mask, h_ref[:, j : j + 2 * BL], jnp.zeros((), bf16))
        ml = jnp.where(mask, l_ref[:, j : j + 2 * BL], jnp.zeros((), bf16))
        th = th_ref[j:n, :]
        tl = tl_ref[j:n, :]
        prod = dot_nn(th, mh) + (dot_nn(th, ml) + dot_nn(tl, mh))
        for i in range(j, n, BL):
            for c in (j, j + BL):
                if i >= c:
                    p = place[(i // BL, c // BL)]
                    out_ref[0, p * BL : (p + 1) * BL, :] = prod[i - j : i - j + BL, c - j : c - j + BL]


def gram(res, code, n_group, rel):
    rows, n = res.shape
    size = len(blocks(n)) * BL
    return pl.pallas_call(
        lambda *refs: gram_body(rel, *refs),
        grid=(n_group,),
        in_specs=[
            pl.BlockSpec((rows, n), lambda g: (0, 0)),
            pl.BlockSpec((rows, 1), lambda g: (0, 0)),
        ],
        out_specs=pl.BlockSpec((1, size, BL), lambda g: (g, 0, 0)),
        out_shape=jax.ShapeDtypeStruct((n_group, size, BL), f32),
        scratch_shapes=[
            pltpu.VMEM((n, rows), bf16),
            pltpu.VMEM((n, rows), bf16),
            pltpu.VMEM((rows, n), bf16),
            pltpu.VMEM((rows, n), bf16),
        ],
        compiler_params=pltpu.CompilerParams(vmem_limit_bytes=40 << 20),
        cost_estimate=pl.CostEstimate(
            flops=3 * n_group * rows * n * n, bytes_accessed=4 * (rows * n + n_group * size * BL), transcendentals=0
        ),
        name="gram",
    )(res, code)


def diag_group(b, tt, s):
    lane = lax.broadcasted_iota(jnp.int32, (SUB, BL), 1)
    sub = lax.broadcasted_iota(jnp.int32, (SUB, BL), 0)
    base = SUB * s
    rows = [jnp.broadcast_to(b[base + t : base + t + 1, :], (SUB, BL)) for t in range(SUB)]
    schur = {}
    for i in range(SUB):
        for u in range(i + 1):
            schur[i, u] = jnp.broadcast_to(rows[i][:, base + u : base + u + 1], (SUB, BL))
    panel = (lane >= base) & (lane < base + SUB)
    fwd = [jnp.where(panel, jnp.where(lane == base + t, 1.0, 0.0), rows[t]) for t in range(SUB)]
    pivot, inv, mult = [], [], {}
    for t in range(SUB):
        pivot.append(schur[t, t])
        inv.append(1.0 / schur[t, t])
        for i in range(t + 1, SUB):
            mult[i, t] = schur[i, t] * inv[t]
        for u in range(t + 1, SUB):
            for i in range(u, SUB):
                schur[i, u] = schur[i, u] - mult[u, t] * schur[i, t]
        for i in range(t + 1, SUB):
            fwd[i] = fwd[i] - mult[i, t] * fwd[t]
    back = [None] * SUB
    for t in reversed(range(SUB)):
        w = fwd[t] * inv[t]
        for i in range(SUB - 1, t, -1):
            w = w - mult[i, t] * back[i]
        back[t] = w
    for g in range(s + 1, BL // SUB):
        x = b[SUB * g : SUB * g + SUB, :]
        even, odd = 0.0, 0.0
        for u in range(0, SUB, 2):
            even = even + jnp.broadcast_to(x[:, base + u : base + u + 1], (SUB, BL)) * back[u]
            odd = odd + jnp.broadcast_to(x[:, base + u + 1 : base + u + 2], (SUB, BL)) * back[u + 1]
        b[SUB * g : SUB * g + SUB, :] = jnp.where(panel, 0.0, x) - (even + odd)
    out = jnp.zeros((SUB, BL), f32)
    for t in range(SUB):
        row = jnp.where(lane <= base + t, fwd[t] * lax.rsqrt(pivot[t]), 0.0)
        out = jnp.where(sub == t, row, out)
    tt[base : base + SUB, :] = out


def chol_body(n, scale_ref, pa_ref, pb_ref, out_ref, w_ref, b_ref, t_ref, h1_ref, h2_ref):
    nb = n // BL
    order = blocks(n)
    place = {b: p for p, b in enumerate(order)}
    half = len(order) // 2
    scale = scale_ref[0]
    row = lax.broadcasted_iota(jnp.int32, (BL, BL), 0)
    col = lax.broadcasted_iota(jnp.int32, (BL, BL), 1)
    for p, (i, j) in enumerate(order):
        src, q = (pa_ref, p) if p < half else (pb_ref, p - half)
        x = src[q * BL : (q + 1) * BL, :] * scale
        if i == j:
            x = x + jnp.where(row == col, ridge, 0.0)
        w_ref[i * BL : (i + 1) * BL, j * BL : (j + 1) * BL] = x

    @pl.loop(0, nb)
    def _(k):
        o = pl.multiple_of(k * BL, BL)
        b_ref[...] = w_ref[pl.ds(o, BL), pl.ds(o, BL)]
        for s in range(BL // SUB):
            diag_group(b_ref, t_ref, s)
        out_ref[pl.ds(pl.multiple_of((len(order) + k) * BL, BL), BL), :] = t_ref[...]
        for kk in range(nb):

            @pl.when(k == kk)
            def _():
                c = kk * BL
                if kk % 2:
                    p = place[(kk, kk - 1)] * BL
                    q = (len(order) + kk - 1) * BL
                    x = dot3(out_ref[p : p + BL, :], out_ref[q : q + BL, :])
                    q = (len(order) + nb + kk // 2) * BL
                    out_ref[q : q + BL, :] = -dot3(t_ref[...], x)
                th, tl = split(t_ref[...])
                tcat = jnp.concatenate([th, tl, th, tl], axis=1)
                for i in range(c, n, BL):
                    ah, al = split(w_ref[i : i + BL, c : c + BL])
                    x = dot_nt(jnp.concatenate([ah, ah, al, al], axis=1), tcat)
                    if i == c:
                        x = jnp.where(row >= col, x, 0.0)
                    p = place[(i // BL, kk)]
                    out_ref[p * BL : (p + 1) * BL, :] = x
                    if i > c:
                        xh, xl = split(x)
                        h1_ref[i : i + BL, :] = jnp.concatenate([xh, xh, xl, xl], axis=1)
                        h2_ref[i : i + BL, :] = jnp.concatenate([xh, xl, xh, xl], axis=1)
                j = c + BL
                while j < n:
                    wide = BL if (j // BL) % 2 == 1 else 2 * BL
                    w_ref[j:n, j : j + wide] = w_ref[j:n, j : j + wide] - dot_nt(
                        h1_ref[j:n, :], h2_ref[j : j + wide, :]
                    )
                    j += wide


def chol(pa, pb, scale, n):
    size = len(blocks(n)) * BL
    return pl.pallas_call(
        lambda *refs: chol_body(n, *refs),
        in_specs=[
            pl.BlockSpec(memory_space=pltpu.SMEM),
            pl.BlockSpec(memory_space=pltpu.VMEM),
            pl.BlockSpec(memory_space=pltpu.VMEM),
        ],
        out_specs=pl.BlockSpec(memory_space=pltpu.VMEM),
        out_shape=jax.ShapeDtypeStruct((size + n + n // 2, BL), f32),
        scratch_shapes=[
            pltpu.VMEM((n, n), f32),
            pltpu.VMEM((BL, BL), f32),
            pltpu.VMEM((BL, BL), f32),
            pltpu.VMEM((n, 4 * BL), bf16),
            pltpu.VMEM((n, 4 * BL), bf16),
        ],
        compiler_params=pltpu.CompilerParams(vmem_limit_bytes=40 << 20),
        cost_estimate=pl.CostEstimate(flops=40 * n * n * n, bytes_accessed=8 * size * BL, transcendentals=0),
        name="chol",
    )(scale, pa, pb)


def whiten_body(n, chunks, *refs):
    mine_ref, own_ref, other_ref = refs[:3]
    res_refs = refs[3 : 3 + chunks]
    tag_refs = refs[3 + chunks : 3 + 2 * chunks]
    out_ref, fac_ref, f_ref, o_ref, lh_ref, ll_ref, th_ref, tl_ref, wh_ref, wl_ref, sem = refs[3 + 2 * chunks :]
    order = blocks(n)
    nb = n // BL
    wide = 2 * BL
    mine = mine_ref[0]
    sources, part, _ = res_refs[0].shape
    rows = sources * part
    copies = []

    for slot, (src, dst) in enumerate(((own_ref, mine), (other_ref, 1 - mine))):
        f_ref[slot] = jnp.zeros((n, n), f32)
        for p, (i, j) in enumerate(order):
            x = src[p * BL : (p + 1) * BL, :]
            f_ref[slot, i * BL : (i + 1) * BL, j * BL : (j + 1) * BL] = x
            hi, lo = split(x)
            lh_ref[slot, i * BL : (i + 1) * BL, j * BL : (j + 1) * BL] = hi
            ll_ref[slot, i * BL : (i + 1) * BL, j * BL : (j + 1) * BL] = lo
        copies.append(pltpu.make_async_copy(f_ref.at[slot], fac_ref.at[dst], sem.at[slot]))
        copies[-1].start()
        for k in range(nb):
            p = (len(order) + k) * BL
            c = (k % 2) * BL
            hi, lo = split(src[p : p + BL, :])
            th_ref[slot, k * BL : (k + 1) * BL, c : c + BL] = hi
            tl_ref[slot, k * BL : (k + 1) * BL, c : c + BL] = lo
            if k % 2:
                p = (len(order) + nb + k // 2) * BL
                hi, lo = split(src[p : p + BL, :])
            else:
                hi = lo = jnp.zeros((BL, BL), bf16)
            th_ref[slot, k * BL : (k + 1) * BL, BL - c : wide - c] = hi
            tl_ref[slot, k * BL : (k + 1) * BL, BL - c : wide - c] = lo

    for c in range(0, n, wide):
        for slot in range(2):
            which = mine if slot == 0 else 1 - mine
            prod = None
            if c:
                lh = lh_ref[slot, c : c + wide, :c]
                ll = ll_ref[slot, c : c + wide, :c]
                wh = wh_ref[slot, :, :c]
                wl = wl_ref[slot, :, :c]
                prod = dot_nt(wh, lh) + (dot_nt(wh, ll) + dot_nt(wl, lh))
            accs = []
            for q in range(chunks):
                x = res_refs[q][:, :, c : c + wide].reshape(rows, wide)
                x = jnp.where(tag_refs[q][...] == which + 1, x, 0.0)
                if prod is not None:
                    x = x - prod[q * rows : (q + 1) * rows]
                accs.append(x)
            ah, al = split(jnp.concatenate(accs, axis=0) if chunks > 1 else accs[0])
            th = th_ref[slot, c : c + wide, :]
            tl = tl_ref[slot, c : c + wide, :]
            x = dot_nt(ah, th) + (dot_nt(ah, tl) + dot_nt(al, th))
            hi, lo = split(x)
            wh_ref[slot, :, c : c + wide] = hi
            wl_ref[slot, :, c : c + wide] = lo
            for q in range(chunks):
                y = x[q * rows : (q + 1) * rows].reshape(sources, part, wide)
                if slot:
                    y = y + o_ref[q, :, :, c : c + wide]
                o_ref[q, :, :, c : c + wide] = y
        for q in range(chunks):
            copies.append(
                pltpu.make_async_copy(
                    o_ref.at[q, :, :, pl.ds(c, wide)],
                    out_ref.at[:, pl.ds(q * part, part), pl.ds(c, wide)],
                    sem.at[2 + (c // wide) * chunks + q],
                )
            )
            copies[-1].start()
    for copy in copies:
        copy.wait()


def whiten(res, tags, own, other, mine):
    chunks = len(res)
    sources, part, n = res[0].shape
    rows = chunks * sources * part
    vmem = pl.BlockSpec(memory_space=pltpu.VMEM)
    hbm = pl.BlockSpec(memory_space=pl.ANY)
    return pl.pallas_call(
        lambda *refs: whiten_body(n, chunks, *refs),
        in_specs=[pl.BlockSpec(memory_space=pltpu.SMEM)] + [vmem] * (2 + 2 * chunks),
        out_specs=[hbm, hbm],
        out_shape=[
            jax.ShapeDtypeStruct((sources, chunks * part, n), f32),
            jax.ShapeDtypeStruct((2, n, n), f32),
        ],
        scratch_shapes=[
            pltpu.VMEM((2, n, n), f32),
            pltpu.VMEM((chunks, sources, part, n), f32),
            pltpu.VMEM((2, n, n), bf16),
            pltpu.VMEM((2, n, n), bf16),
            pltpu.VMEM((2, n, 2 * BL), bf16),
            pltpu.VMEM((2, n, 2 * BL), bf16),
            pltpu.VMEM((2, rows, n), bf16),
            pltpu.VMEM((2, rows, n), bf16),
            pltpu.SemaphoreType.DMA((2 + chunks * (n // (2 * BL)),)),
        ],
        compiler_params=pltpu.CompilerParams(vmem_limit_bytes=58 << 20),
        cost_estimate=pl.CostEstimate(flops=12 * rows * n * n, bytes_accessed=16 * n * n, transcendentals=0),
        name="whiten",
    )(mine, own, other, *res, *tags)


def flip(x, axis, bit):
    size = lax.axis_size(axis)
    return lax.ppermute(x, axis, [(i, i ^ (1 << bit)) for i in range(size)])


def bit_of(axis, bit):
    return (lax.axis_index(axis) >> bit) & 1


def halve(x, axis, bit, dim):
    b = bit_of(axis, bit)
    got = flip(lax.dynamic_slice_in_dim(x, 1 - b, 1, dim), axis, bit)
    return lax.dynamic_slice_in_dim(x, b, 1, dim) + got


def double(x, axis, bit, dim):
    got = flip(x, axis, bit)
    low = bit_of(axis, bit) == 0
    return jnp.where(low, jnp.concatenate([x, got], dim), jnp.concatenate([got, x], dim))


def sum_and_share(part, n_group, n_member):
    gbits = n_group.bit_length() - 1
    mbits = n_member.bit_length() - 1
    rows = part.shape[1]
    shape = (2,) * gbits + (2,) * (mbits - 1)
    ghalf = [("group", b, gbits - 1 - b) for b in range(gbits)]
    mhalf = [("member", b, gbits + b - 1) for b in range(1, mbits)]
    plans = [ghalf + mhalf, mhalf[:1] + ghalf + mhalf[1:]]
    gathers = [mhalf[::-1], mhalf[:1] + mhalf[:0:-1]]
    parts = [
        part[:, c * (rows // 2) : (c + 1) * (rows // 2)].reshape(shape + (rows >> mbits, BL)) for c in range(2)
    ]
    for step in range(gbits + mbits - 1):
        parts = [halve(parts[c], *plans[c][step]) for c in range(2)]
    for step in range(mbits - 1):
        parts = [double(parts[c], *gathers[c][step]) for c in range(2)]
    return [p.reshape(rows // 2, BL) for p in parts]


def to_owners(x):
    return lax.all_to_all(x, ("group", "member"), split_axis=0, concat_axis=0, tiled=True)


def on_device(rows, old_list, old_centroids, dest_device, new_local, centroids):
    n_group = lax.axis_size("group")
    n_member = lax.axis_size("member")
    devices = n_group * n_member
    row_dev, width = rows.shape
    lists = centroids.shape[0]
    capacity = max(2, 2 * row_dev // devices)
    group = lax.axis_index("group")
    core = lax.axis_index("member") & 1

    every = jnp.zeros((n_group,) + centroids.shape, f32)
    for shift in range(n_group):
        got = centroids
        if shift:
            got = lax.ppermute(centroids, "group", [(i, (i + shift) % n_group) for i in range(n_group)])
        every = lax.dynamic_update_index_in_dim(every, got, (group - shift) % n_group, 0)
    every = every.reshape(n_group * lists, width)

    dest = dest_device[:, 0]
    new_list = (dest // n_member) * lists + new_local
    old_hot = (old_list[:, None] == jnp.arange(old_centroids.shape[0], dtype=jnp.int32)[None, :]).astype(f32)
    new_hot = (new_list[:, None] == jnp.arange(n_group * lists, dtype=jnp.int32)[None, :]).astype(f32)
    vectors = rows + jnp.dot(old_hot, old_centroids, precision=lax.Precision.HIGHEST)
    residual = vectors - jnp.dot(new_hot, every, precision=lax.Precision.HIGHEST)

    onehot = (dest[:, None] == jnp.arange(devices, dtype=jnp.int32)[None, :]).astype(jnp.int32)
    ranks = jnp.sum(jnp.cumsum(onehot, axis=0) * onehot, axis=1) - 1
    position = dest * capacity + ranks
    chunk = capacity // 2 if capacity % (2 * SUB) == 0 else capacity
    slot_of = (ranks // chunk) * devices * chunk + dest * chunk + ranks % chunk
    outgoing = jnp.zeros((devices * capacity, width), f32).at[slot_of].set(residual)
    outgoing = outgoing.reshape(capacity // chunk, devices, chunk, width)
    out_tags = jnp.zeros((devices * capacity,), jnp.int32).at[position].set(new_local + 1)
    sent = jnp.sum(new_hot, axis=0).astype(jnp.int32).reshape(n_group, lists)
    info = jnp.concatenate(
        [out_tags.reshape(devices, capacity), jnp.repeat(sent, n_member, axis=0)], axis=1
    ).reshape(devices, 1, -1)

    first = to_owners(outgoing[0])
    code = ((dest // n_member) * 2 + (new_local ^ core))[:, None]
    away = gram(residual, code, n_group, 1)
    part = gram(residual, code, n_group, 0)
    part = part + flip(away, "member", 0)
    info, first = lax.optimization_barrier((info, first))
    info = to_owners(info)[:, 0]
    pa, pb = sum_and_share(part, n_group, n_member)
    arrived = [first]
    for later in outgoing[1:]:
        later, info, pa, pb = lax.optimization_barrier((later, info, pa, pb))
        arrived.append(to_owners(later))
    tags = [info[:, c : c + chunk].reshape(-1, 1) for c in range(0, capacity, chunk)]
    counts = jnp.sum(info[:, capacity:], axis=0).astype(f32)
    count = lax.dynamic_index_in_dim(counts, core, 0, keepdims=True)
    scale = 1.0 / jnp.maximum(count, 1.0)
    own = chol(pa, pb, scale, width)
    other = flip(own, "member", 0)
    result, factors = whiten(arrived, tags, own, other, core.reshape(1))
    return (result.reshape(devices * capacity, width), factors)


def solution(mesh):
    return jax.shard_map(
        on_device,
        mesh=mesh,
        in_specs=(
            P(("group", "member"), None),
            P(("group", "member")),
            P(),
            P(("group", "member"), None),
            P(("group", "member")),
            P("group", None),
        ),
        out_specs=(P(("group", "member"), None), P("group", None, None)),
        check_vma=False,
    )
```

```python
import jax
import jax.numpy as jnp
from jax import lax
from jax.experimental import pallas as pl
from jax.experimental.pallas import tpu as pltpu
from jax.sharding import PartitionSpec as P


ridge = 0.1
f32 = jnp.float32
bf16 = jnp.bfloat16
BL = 128
SUB = 8


def split(x):
    hi = x.astype(bf16)
    return hi, (x - hi.astype(f32)).astype(bf16)


def dot_nt(a, b):
    return lax.dot_general(a, b, (((1,), (1,)), ((), ())), preferred_element_type=f32)


def dot_nn(a, b):
    return lax.dot_general(a, b, (((1,), (0,)), ((), ())), preferred_element_type=f32)


def dot3(a, b):
    ah, al = split(a)
    bh, bl = split(b)
    return dot_nn(ah, bh) + (dot_nn(ah, bl) + dot_nn(al, bh))


def blocks(n):
    nb = n // BL
    return [(i, j) for j in range(nb) for i in range(j, nb)]


def split3(x):
    hi = x.astype(bf16)
    rest = x - hi.astype(f32)
    mid = rest.astype(bf16)
    return hi, mid, (rest - mid.astype(f32)).astype(bf16)


def table_rows(index, table):
    count = table.shape[0]
    hot = (lax.broadcasted_iota(jnp.int32, (count, index.shape[1]), 0) == index).astype(f32)
    hot = jnp.concatenate([hot] * 3, axis=0).astype(bf16)
    return lax.dot_general(
        hot, jnp.concatenate(split3(table), axis=0), (((0,), (0,)), ((), ())), preferred_element_type=f32
    )


def route_body(sizes, ids_ref, rows_ref, old_ref, dest_ref, local_ref, table_ref, *refs):
    n_group, n_member, capacity, chunk = sizes
    devices = n_group * n_member
    chunks = capacity // chunk
    out_refs = refs[:chunks]
    vec_ref, info_ref, code_ref, o_ref, sem = refs[chunks:]
    count, _ = rows_ref.shape
    group, core = ids_ref[0], ids_ref[1]
    dest = dest_ref[...]
    local = local_ref[...]
    shift = n_member.bit_length() - 1
    device = lax.broadcasted_iota(jnp.int32, (devices, count), 0)
    onehot = (device == dest).astype(f32)
    earlier = lax.broadcasted_iota(jnp.int32, (count, count), 0) < lax.broadcasted_iota(jnp.int32, (count, count), 1)
    ahead = dot_nn(onehot.astype(bf16), earlier.astype(f32).astype(bf16))
    rank = jnp.sum(onehot * ahead, axis=0, keepdims=True).astype(jnp.int32)
    low = chunk.bit_length() - 1
    place = (rank >> low) * (devices * chunk) + dest * chunk + (rank & (chunk - 1))

    to_group = dest >> shift
    row = lax.broadcasted_iota(jnp.int32, (SUB, count), 0)
    code = to_group * 2 + (local ^ core)
    seen = ((group - to_group) & (n_group - 1)) * 2 + local
    code_ref[...] = jnp.where(row == 0, code, seen)

    slot = lax.broadcasted_iota(jnp.int32, (BL, count), 0)
    left = jnp.concatenate(
        [onehot * (local + 1).astype(f32), ((device >> shift) == to_group).astype(f32)], axis=1
    )
    right = jnp.concatenate(
        [((slot == rank) & (slot < capacity)).astype(f32), ((slot - capacity) == local).astype(f32)], axis=1
    )
    info_ref[...] = dot_nt(left.astype(bf16), right.astype(bf16)).astype(jnp.int32)

    vec = rows_ref[...] + table_rows(old_ref[...], table_ref[...])
    vec_ref[...] = vec
    hi, mid, lo = split3(vec)
    copies = []
    for q in range(chunks):
        for r in range(0, devices * chunk, 2 * BL):
            base = q * devices * chunk + r
            pick = (lax.broadcasted_iota(jnp.int32, (2 * BL, count), 0) + base == place).astype(f32).astype(bf16)
            o_ref[base : base + 2 * BL, :] = dot_nn(pick, hi) + (dot_nn(pick, mid) + dot_nn(pick, lo))
            copies.append(
                pltpu.make_async_copy(
                    o_ref.at[pl.ds(base, 2 * BL), :], out_refs[q].at[pl.ds(r, 2 * BL), :], sem.at[base // (2 * BL)]
                )
            )
            copies[-1].start()
    for copy in copies:
        copy.wait()


def route(ids, rows, old, dest, local, table, sizes):
    n_group, n_member, capacity, chunk = sizes
    devices = n_group * n_member
    count, n = rows.shape
    chunks = capacity // chunk
    vmem = pl.BlockSpec(memory_space=pltpu.VMEM)
    return pl.pallas_call(
        lambda *refs: route_body(sizes, *refs),
        in_specs=[pl.BlockSpec(memory_space=pltpu.SMEM)] + [vmem] * 5,
        out_specs=[pl.BlockSpec(memory_space=pl.ANY)] * chunks + [vmem] * 3,
        out_shape=[jax.ShapeDtypeStruct((devices * chunk, n), f32)] * chunks
        + [
            jax.ShapeDtypeStruct((count, n), f32),
            jax.ShapeDtypeStruct((devices, BL), jnp.int32),
            jax.ShapeDtypeStruct((SUB, count), jnp.int32),
        ],
        scratch_shapes=[
            pltpu.VMEM((devices * capacity, n), f32),
            pltpu.SemaphoreType.DMA((devices * capacity // (2 * BL),)),
        ],
        compiler_params=pltpu.CompilerParams(vmem_limit_bytes=40 << 20),
        cost_estimate=pl.CostEstimate(
            flops=6 * devices * capacity * count * n, bytes_accessed=4 * devices * capacity * n, transcendentals=0
        ),
        name="route",
    )(ids, rows, old, dest, local, table)


def gram_body(rel, vec_ref, code_ref, table_ref, a_ref, b_ref, th_ref, tl_ref, h_ref, l_ref):
    g = pl.program_id(0)
    _, n = vec_ref.shape
    order = blocks(n)
    half = len(order) // 2

    @pl.when(g == 0)
    def _():
        x = vec_ref[...] - table_rows(code_ref[1:2, :], table_ref[...])
        hi, lo = split(x)
        h_ref[...] = hi
        l_ref[...] = lo
        for j in range(0, n, BL):
            hi, lo = split(x[:, j : j + BL].T)
            th_ref[j : j + BL, :] = hi
            tl_ref[j : j + BL, :] = lo

    mask = (code_ref[0:1, :] == 2 * g + rel).astype(f32).astype(bf16)
    place = {b: p for p, b in enumerate(order)}
    for j in range(0, n, 2 * BL):
        mh = h_ref[:, j : j + 2 * BL]
        ml = l_ref[:, j : j + 2 * BL]
        th = th_ref[j:n, :] * mask
        tl = tl_ref[j:n, :] * mask
        prod = dot_nn(th, mh) + (dot_nn(th, ml) + dot_nn(tl, mh))
        for i in range(j, n, BL):
            for c in (j, j + BL):
                if i >= c:
                    p = place[(i // BL, c // BL)]
                    dst, p = (a_ref, p) if p < half else (b_ref, p - half)
                    dst[0, p * BL : (p + 1) * BL, :] = prod[i - j : i - j + BL, c - j : c - j + BL]


def gram(vec, code, table, n_group, rel):
    rows, n = vec.shape
    size = len(blocks(n)) * BL // 2
    return pl.pallas_call(
        lambda *refs: gram_body(rel, *refs),
        grid=(n_group,),
        in_specs=[
            pl.BlockSpec((rows, n), lambda g: (0, 0)),
            pl.BlockSpec(code.shape, lambda g: (0, 0)),
            pl.BlockSpec(table.shape, lambda g: (0, 0)),
        ],
        out_specs=[pl.BlockSpec((1, size, BL), lambda g: (g, 0, 0))] * 2,
        out_shape=[jax.ShapeDtypeStruct((n_group, size, BL), f32)] * 2,
        scratch_shapes=[
            pltpu.VMEM((n, rows), bf16),
            pltpu.VMEM((n, rows), bf16),
            pltpu.VMEM((rows, n), bf16),
            pltpu.VMEM((rows, n), bf16),
        ],
        compiler_params=pltpu.CompilerParams(vmem_limit_bytes=40 << 20),
        cost_estimate=pl.CostEstimate(
            flops=3 * n_group * rows * n * n, bytes_accessed=4 * (rows * n + 2 * n_group * size * BL), transcendentals=0
        ),
        name="gram",
    )(vec, code, table)


def diag_group(b, tt, s):
    lane = lax.broadcasted_iota(jnp.int32, (SUB, BL), 1)
    sub = lax.broadcasted_iota(jnp.int32, (SUB, BL), 0)
    base = SUB * s
    rows = [jnp.broadcast_to(b[base + t : base + t + 1, :], (SUB, BL)) for t in range(SUB)]
    schur = {}
    for i in range(SUB):
        for u in range(i + 1):
            schur[i, u] = jnp.broadcast_to(rows[i][:, base + u : base + u + 1], (SUB, BL))
    panel = (lane >= base) & (lane < base + SUB)
    fwd = [jnp.where(panel, jnp.where(lane == base + t, 1.0, 0.0), rows[t]) for t in range(SUB)]
    pivot, inv, mult = [], [], {}
    for t in range(SUB):
        pivot.append(schur[t, t])
        inv.append(1.0 / schur[t, t])
        for i in range(t + 1, SUB):
            mult[i, t] = schur[i, t] * inv[t]
        for u in range(t + 1, SUB):
            for i in range(u, SUB):
                schur[i, u] = schur[i, u] - mult[u, t] * schur[i, t]
        for i in range(t + 1, SUB):
            fwd[i] = fwd[i] - mult[i, t] * fwd[t]
    back = [None] * SUB
    for t in reversed(range(SUB)):
        w = fwd[t] * inv[t]
        for i in range(SUB - 1, t, -1):
            w = w - mult[i, t] * back[i]
        back[t] = w
    for g in range(s + 1, BL // SUB):
        x = b[SUB * g : SUB * g + SUB, :]
        even, odd = 0.0, 0.0
        for u in range(0, SUB, 2):
            even = even + jnp.broadcast_to(x[:, base + u : base + u + 1], (SUB, BL)) * back[u]
            odd = odd + jnp.broadcast_to(x[:, base + u + 1 : base + u + 2], (SUB, BL)) * back[u + 1]
        b[SUB * g : SUB * g + SUB, :] = jnp.where(panel, 0.0, x) - (even + odd)
    out = jnp.zeros((SUB, BL), f32)
    for t in range(SUB):
        row = jnp.where(lane <= base + t, fwd[t] * lax.rsqrt(pivot[t]), 0.0)
        out = jnp.where(sub == t, row, out)
    tt[base : base + SUB, :] = out


def chol_body(n, scale_ref, pa_ref, pb_ref, out_ref, w_ref, b_ref, t_ref, h1_ref, h2_ref):
    nb = n // BL
    order = blocks(n)
    place = {b: p for p, b in enumerate(order)}
    half = len(order) // 2
    scale = scale_ref[0]
    row = lax.broadcasted_iota(jnp.int32, (BL, BL), 0)
    col = lax.broadcasted_iota(jnp.int32, (BL, BL), 1)
    for p, (i, j) in enumerate(order):
        src, q = (pa_ref, p) if p < half else (pb_ref, p - half)
        x = src[q * BL : (q + 1) * BL, :] * scale
        if i == j:
            x = x + jnp.where(row == col, ridge, 0.0)
        w_ref[i * BL : (i + 1) * BL, j * BL : (j + 1) * BL] = x

    @pl.loop(0, nb)
    def _(k):
        o = pl.multiple_of(k * BL, BL)
        b_ref[...] = w_ref[pl.ds(o, BL), pl.ds(o, BL)]
        for s in range(BL // SUB):
            diag_group(b_ref, t_ref, s)
        out_ref[pl.ds(pl.multiple_of((len(order) + k) * BL, BL), BL), :] = t_ref[...]
        for kk in range(nb):

            @pl.when(k == kk)
            def _():
                c = kk * BL
                if kk % 2:
                    p = place[(kk, kk - 1)] * BL
                    q = (len(order) + kk - 1) * BL
                    x = dot3(out_ref[p : p + BL, :], out_ref[q : q + BL, :])
                    q = (len(order) + nb + kk // 2) * BL
                    out_ref[q : q + BL, :] = -dot3(t_ref[...], x)
                th, tl = split(t_ref[...])
                tcat = jnp.concatenate([th, tl, th, tl], axis=1)
                for i in range(c, n, BL):
                    ah, al = split(w_ref[i : i + BL, c : c + BL])
                    x = dot_nt(jnp.concatenate([ah, ah, al, al], axis=1), tcat)
                    if i == c:
                        x = jnp.where(row >= col, x, 0.0)
                    p = place[(i // BL, kk)]
                    out_ref[p * BL : (p + 1) * BL, :] = x
                    if i > c:
                        xh, xl = split(x)
                        h1_ref[i : i + BL, :] = jnp.concatenate([xh, xh, xl, xl], axis=1)
                        h2_ref[i : i + BL, :] = jnp.concatenate([xh, xl, xh, xl], axis=1)
                j = c + BL
                while j < n:
                    wide = BL if (j // BL) % 2 == 1 else 2 * BL
                    w_ref[j:n, j : j + wide] = w_ref[j:n, j : j + wide] - dot_nt(
                        h1_ref[j:n, :], h2_ref[j : j + wide, :]
                    )
                    j += wide


def chol(pa, pb, scale, n):
    size = len(blocks(n)) * BL
    return pl.pallas_call(
        lambda *refs: chol_body(n, *refs),
        in_specs=[
            pl.BlockSpec(memory_space=pltpu.SMEM),
            pl.BlockSpec(memory_space=pltpu.VMEM),
            pl.BlockSpec(memory_space=pltpu.VMEM),
        ],
        out_specs=pl.BlockSpec(memory_space=pltpu.VMEM),
        out_shape=jax.ShapeDtypeStruct((size + n + n // 2, BL), f32),
        scratch_shapes=[
            pltpu.VMEM((n, n), f32),
            pltpu.VMEM((BL, BL), f32),
            pltpu.VMEM((BL, BL), f32),
            pltpu.VMEM((n, 4 * BL), bf16),
            pltpu.VMEM((n, 4 * BL), bf16),
        ],
        compiler_params=pltpu.CompilerParams(vmem_limit_bytes=40 << 20),
        cost_estimate=pl.CostEstimate(flops=40 * n * n * n, bytes_accessed=8 * size * BL, transcendentals=0),
        name="chol",
    )(scale, pa, pb)


def whiten_body(n, chunks, *refs):
    mine_ref, cent_ref, own_ref, other_ref = refs[:4]
    res_refs = refs[4 : 4 + chunks]
    tag_refs = refs[4 + chunks : 4 + 2 * chunks]
    out_ref, fac_ref, f_ref, o_ref, lh_ref, ll_ref, th_ref, tl_ref, wh_ref, wl_ref, sem = refs[4 + 2 * chunks :]
    order = blocks(n)
    nb = n // BL
    wide = 2 * BL
    mine = mine_ref[0]
    sources, part, _ = res_refs[0].shape
    rows = sources * part
    copies = []

    for slot, (src, dst) in enumerate(((own_ref, mine), (other_ref, 1 - mine))):
        f_ref[slot] = jnp.zeros((n, n), f32)
        for p, (i, j) in enumerate(order):
            x = src[p * BL : (p + 1) * BL, :]
            f_ref[slot, i * BL : (i + 1) * BL, j * BL : (j + 1) * BL] = x
            hi, lo = split(x)
            lh_ref[slot, i * BL : (i + 1) * BL, j * BL : (j + 1) * BL] = hi
            ll_ref[slot, i * BL : (i + 1) * BL, j * BL : (j + 1) * BL] = lo
        copies.append(pltpu.make_async_copy(f_ref.at[slot], fac_ref.at[dst], sem.at[slot]))
        copies[-1].start()
        for k in range(nb):
            p = (len(order) + k) * BL
            c = (k % 2) * BL
            hi, lo = split(src[p : p + BL, :])
            th_ref[slot, k * BL : (k + 1) * BL, c : c + BL] = hi
            tl_ref[slot, k * BL : (k + 1) * BL, c : c + BL] = lo
            if k % 2:
                p = (len(order) + nb + k // 2) * BL
                hi, lo = split(src[p : p + BL, :])
            else:
                hi = lo = jnp.zeros((BL, BL), bf16)
            th_ref[slot, k * BL : (k + 1) * BL, BL - c : wide - c] = hi
            tl_ref[slot, k * BL : (k + 1) * BL, BL - c : wide - c] = lo

    for c in range(0, n, wide):
        for slot in range(2):
            which = mine if slot == 0 else 1 - mine
            prod = None
            if c:
                lh = lh_ref[slot, c : c + wide, :c]
                ll = ll_ref[slot, c : c + wide, :c]
                wh = wh_ref[slot, :, :c]
                wl = wl_ref[slot, :, :c]
                prod = dot_nt(wh, lh) + (dot_nt(wh, ll) + dot_nt(wl, lh))
            accs = []
            for q in range(chunks):
                x = res_refs[q][:, :, c : c + wide].reshape(rows, wide)
                x = jnp.where(tag_refs[q][...] == which + 1, x - cent_ref[pl.ds(which, 1), c : c + wide], 0.0)
                if prod is not None:
                    x = x - prod[q * rows : (q + 1) * rows]
                accs.append(x)
            ah, al = split(jnp.concatenate(accs, axis=0) if chunks > 1 else accs[0])
            th = th_ref[slot, c : c + wide, :]
            tl = tl_ref[slot, c : c + wide, :]
            x = dot_nt(ah, th) + (dot_nt(ah, tl) + dot_nt(al, th))
            hi, lo = split(x)
            wh_ref[slot, :, c : c + wide] = hi
            wl_ref[slot, :, c : c + wide] = lo
            for q in range(chunks):
                y = x[q * rows : (q + 1) * rows].reshape(sources, part, wide)
                if slot:
                    y = y + o_ref[q, :, :, c : c + wide]
                o_ref[q, :, :, c : c + wide] = y
        for q in range(chunks):
            copies.append(
                pltpu.make_async_copy(
                    o_ref.at[q, :, :, pl.ds(c, wide)],
                    out_ref.at[:, pl.ds(q * part, part), pl.ds(c, wide)],
                    sem.at[2 + (c // wide) * chunks + q],
                )
            )
            copies[-1].start()
    for copy in copies:
        copy.wait()


def whiten(res, tags, own, other, mine, centroids):
    chunks = len(res)
    sources, part, n = res[0].shape
    rows = chunks * sources * part
    vmem = pl.BlockSpec(memory_space=pltpu.VMEM)
    hbm = pl.BlockSpec(memory_space=pl.ANY)
    return pl.pallas_call(
        lambda *refs: whiten_body(n, chunks, *refs),
        in_specs=[pl.BlockSpec(memory_space=pltpu.SMEM)] + [vmem] * (3 + 2 * chunks),
        out_specs=[hbm, hbm],
        out_shape=[
            jax.ShapeDtypeStruct((sources, chunks * part, n), f32),
            jax.ShapeDtypeStruct((2, n, n), f32),
        ],
        scratch_shapes=[
            pltpu.VMEM((2, n, n), f32),
            pltpu.VMEM((chunks, sources, part, n), f32),
            pltpu.VMEM((2, n, n), bf16),
            pltpu.VMEM((2, n, n), bf16),
            pltpu.VMEM((2, n, 2 * BL), bf16),
            pltpu.VMEM((2, n, 2 * BL), bf16),
            pltpu.VMEM((2, rows, n), bf16),
            pltpu.VMEM((2, rows, n), bf16),
            pltpu.SemaphoreType.DMA((2 + chunks * (n // (2 * BL)),)),
        ],
        compiler_params=pltpu.CompilerParams(vmem_limit_bytes=58 << 20),
        cost_estimate=pl.CostEstimate(flops=12 * rows * n * n, bytes_accessed=16 * n * n, transcendentals=0),
        name="whiten",
    )(mine, centroids, own, other, *res, *tags)


def flip(x, axis, bit):
    size = lax.axis_size(axis)
    return lax.ppermute(x, axis, [(i, i ^ (1 << bit)) for i in range(size)])


def bit_of(axis, bit):
    return (lax.axis_index(axis) >> bit) & 1


def halve(x, axis, bit, dim):
    b = bit_of(axis, bit)
    got = flip(lax.dynamic_slice_in_dim(x, 1 - b, 1, dim), axis, bit)
    return lax.dynamic_slice_in_dim(x, b, 1, dim) + got


def double(x, axis, bit, dim):
    got = flip(x, axis, bit)
    low = bit_of(axis, bit) == 0
    return jnp.where(low, jnp.concatenate([x, got], dim), jnp.concatenate([got, x], dim))


def sum_and_share(parts, n_group, n_member):
    gbits = n_group.bit_length() - 1
    mbits = n_member.bit_length() - 1
    rows = parts[0].shape[1]
    shape = (2,) * gbits + (2,) * (mbits - 1)
    ghalf = [("group", b, gbits - 1 - b) for b in range(gbits)]
    mhalf = [("member", b, gbits + b - 1) for b in range(1, mbits)]
    plans = [ghalf + mhalf, mhalf[:1] + ghalf + mhalf[1:]]
    gathers = [mhalf[::-1], mhalf[:1] + mhalf[:0:-1]]
    parts = [p.reshape(shape + (rows >> (mbits - 1), BL)) for p in parts]
    for step in range(gbits + mbits - 1):
        parts = [halve(parts[c], *plans[c][step]) for c in range(2)]
    for step in range(mbits - 1):
        parts = [double(parts[c], *gathers[c][step]) for c in range(2)]
    return [p.reshape(rows, BL) for p in parts]


def to_owners(x):
    return lax.all_to_all(x, ("group", "member"), split_axis=0, concat_axis=0, tiled=True)


def on_device(rows, old_list, old_centroids, dest_device, new_local, centroids):
    n_group = lax.axis_size("group")
    n_member = lax.axis_size("member")
    devices = n_group * n_member
    row_dev, width = rows.shape
    lists = centroids.shape[0]
    capacity = max(2, 2 * row_dev // devices)
    group = lax.axis_index("group")
    core = lax.axis_index("member") & 1

    seen = [centroids]
    for shift in range(1, n_group):
        seen.append(lax.ppermute(centroids, "group", [(i, (i + shift) % n_group) for i in range(n_group)]))
    spare = -(n_group * lists) % SUB
    seen = jnp.concatenate(seen + [jnp.zeros((spare, width), f32)] * (spare > 0), axis=0)

    chunk = capacity // 2 if capacity % (2 * SUB) == 0 else capacity
    *outgoing, vectors, info, code = route(
        jnp.stack([group, core]),
        rows,
        old_list.reshape(1, -1),
        dest_device.reshape(1, -1),
        new_local.reshape(1, -1),
        old_centroids,
        (n_group, n_member, capacity, chunk),
    )
    outgoing = [x.reshape(devices, chunk, width) for x in outgoing]

    first = to_owners(outgoing[0])
    away = gram(vectors, code, seen, n_group, 1)
    kept = gram(vectors, code, seen, n_group, 0)
    parts = [k + flip(x, "member", 0) for k, x in zip(kept, away)]
    info, first = lax.optimization_barrier((info.reshape(devices, 1, BL), first))
    info = to_owners(info)[:, 0]
    pa, pb = sum_and_share(parts, n_group, n_member)
    tags = [info[:, c : c + chunk].reshape(-1, 1) for c in range(0, capacity, chunk)]
    counts = jnp.sum(info[:, capacity : capacity + lists], axis=0).astype(f32)
    count = lax.dynamic_index_in_dim(counts, core, 0, keepdims=True)
    scale = 1.0 / jnp.maximum(count, 1.0)
    arrived = [first]
    for later in outgoing[1:]:
        later, scale, pa, pb = lax.optimization_barrier((later, scale, pa, pb))
        arrived.append(to_owners(later))
    own = chol(pa, pb, scale, width)
    other = flip(own, "member", 0)
    result, factors = whiten(arrived, tags, own, other, core.reshape(1), centroids)
    return (result.reshape(devices * capacity, width), factors)


def solution(mesh):
    return jax.shard_map(
        on_device,
        mesh=mesh,
        in_specs=(
            P(("group", "member"), None),
            P(("group", "member")),
            P(),
            P(("group", "member"), None),
            P(("group", "member")),
            P("group", None),
        ),
        out_specs=(P(("group", "member"), None), P("group", None, None)),
        check_vma=False,
    )
```

```python
import jax
import jax.numpy as jnp
from jax import lax
from jax.experimental import pallas as pl
from jax.experimental.pallas import tpu as pltpu
from jax.sharding import PartitionSpec as P


ridge = 0.1
f32 = jnp.float32
bf16 = jnp.bfloat16
BL = 128
SUB = 8
NEST = 8


def split(x):
    hi = x.astype(bf16)
    return hi, (x - hi.astype(f32)).astype(bf16)


def dot_nt(a, b):
    return lax.dot_general(a, b, (((1,), (1,)), ((), ())), preferred_element_type=f32)


def dot_nn(a, b):
    return lax.dot_general(a, b, (((1,), (0,)), ((), ())), preferred_element_type=f32)


def dot3(a, b):
    ah, al = split(a)
    bh, bl = split(b)
    return dot_nn(ah, bh) + (dot_nn(ah, bl) + dot_nn(al, bh))


def blocks(n):
    nb = n // BL
    return [(i, j) for j in range(nb) for i in range(j, nb)]


def split3(x):
    hi = x.astype(bf16)
    rest = x - hi.astype(f32)
    mid = rest.astype(bf16)
    return hi, mid, (rest - mid.astype(f32)).astype(bf16)


def table_rows(index, table):
    count = table.shape[0]
    hot = (lax.broadcasted_iota(jnp.int32, (count, index.shape[1]), 0) == index).astype(f32)
    hot = jnp.concatenate([hot] * 3, axis=0).astype(bf16)
    return lax.dot_general(
        hot, jnp.concatenate(split3(table), axis=0), (((0,), (0,)), ((), ())), preferred_element_type=f32
    )


def route_body(sizes, ids_ref, rows_hbm, old_ref, dest_ref, local_ref, table_hbm, *refs):
    n_group, n_member, capacity, chunk = sizes
    devices = n_group * n_member
    chunks = capacity // chunk
    out_refs = refs[:chunks]
    vec_hbm, info_ref, code_ref, rows_ref, table_ref, vec_ref, o_ref, sem = refs[chunks:]
    count, _ = rows_ref.shape
    loads = [
        pltpu.make_async_copy(rows_hbm, rows_ref, sem.at[0]),
        pltpu.make_async_copy(table_hbm, table_ref, sem.at[1]),
    ]
    for copy in loads:
        copy.start()
    group, core = ids_ref[0], ids_ref[1]
    dest = dest_ref[...]
    local = local_ref[...]
    shift = n_member.bit_length() - 1
    device = lax.broadcasted_iota(jnp.int32, (devices, count), 0)
    onehot = (device == dest).astype(f32)
    earlier = lax.broadcasted_iota(jnp.int32, (count, count), 0) < lax.broadcasted_iota(jnp.int32, (count, count), 1)
    ahead = dot_nn(onehot.astype(bf16), earlier.astype(f32).astype(bf16))
    rank = jnp.sum(onehot * ahead, axis=0, keepdims=True).astype(jnp.int32)
    low = chunk.bit_length() - 1
    place = (rank >> low) * (devices * chunk) + dest * chunk + (rank & (chunk - 1))

    to_group = dest >> shift
    row = lax.broadcasted_iota(jnp.int32, (SUB, count), 0)
    code = to_group * 2 + (local ^ core)
    seen = ((group - to_group) & (n_group - 1)) * 2 + local
    code_ref[...] = jnp.where(row == 0, code, seen)

    slot = lax.broadcasted_iota(jnp.int32, (BL, count), 0)
    left = jnp.concatenate(
        [onehot * (local + 1).astype(f32), ((device >> shift) == to_group).astype(f32)], axis=1
    )
    right = jnp.concatenate(
        [((slot == rank) & (slot < capacity)).astype(f32), ((slot - capacity) == local).astype(f32)], axis=1
    )
    info_ref[...] = dot_nt(left.astype(bf16), right.astype(bf16)).astype(jnp.int32)

    for copy in loads:
        copy.wait()
    vec = rows_ref[...] + table_rows(old_ref[...], table_ref[...])
    vec_ref[...] = vec
    hi, mid, lo = split3(vec)
    copies = []
    for q in range(chunks):
        for r in range(0, devices * chunk, 2 * BL):
            base = q * devices * chunk + r
            pick = (lax.broadcasted_iota(jnp.int32, (2 * BL, count), 0) + base == place).astype(f32).astype(bf16)
            o_ref[base : base + 2 * BL, :] = dot_nn(pick, hi) + (dot_nn(pick, mid) + dot_nn(pick, lo))
            copies.append(
                pltpu.make_async_copy(
                    o_ref.at[pl.ds(base, 2 * BL), :], out_refs[q].at[pl.ds(r, 2 * BL), :], sem.at[3 + base // (2 * BL)]
                )
            )
            copies[-1].start()
    copies.append(pltpu.make_async_copy(vec_ref, vec_hbm, sem.at[2]))
    copies[-1].start()
    for copy in copies:
        copy.wait()


def route(ids, rows, old, dest, local, table, sizes):
    n_group, n_member, capacity, chunk = sizes
    devices = n_group * n_member
    count, n = rows.shape
    chunks = capacity // chunk
    vmem = pl.BlockSpec(memory_space=pltpu.VMEM)
    hbm = pl.BlockSpec(memory_space=pltpu.HBM)
    return pl.pallas_call(
        lambda *refs: route_body(sizes, *refs),
        in_specs=[pl.BlockSpec(memory_space=pltpu.SMEM), hbm, vmem, vmem, vmem, hbm],
        out_specs=[hbm] * (chunks + 1) + [vmem] * 2,
        out_shape=[jax.ShapeDtypeStruct((devices * chunk, n), f32)] * chunks
        + [
            jax.ShapeDtypeStruct((count, n), f32),
            jax.ShapeDtypeStruct((devices, BL), jnp.int32),
            jax.ShapeDtypeStruct((SUB, count), jnp.int32),
        ],
        scratch_shapes=[
            pltpu.VMEM((count, n), f32),
            pltpu.VMEM(table.shape, f32),
            pltpu.VMEM((count, n), f32),
            pltpu.VMEM((devices * capacity, n), f32),
            pltpu.SemaphoreType.DMA((3 + devices * capacity // (2 * BL),)),
        ],
        cost_estimate=pl.CostEstimate(
            flops=6 * devices * capacity * count * n, bytes_accessed=4 * devices * capacity * n, transcendentals=0
        ),
        name="route",
    )(ids, rows, old, dest, local, table)


def gram_body(rel, vec_ref, code_ref, table_ref, a_ref, b_ref, t_ref, h_ref):
    g = pl.program_id(0)
    rows, n = vec_ref.shape
    order = blocks(n)
    half = len(order) // 2

    @pl.when(g == 0)
    def _():
        x = vec_ref[...] - table_rows(code_ref[1:2, :], table_ref[...])
        hi, lo = split(x)
        for at, y in enumerate((hi, lo, hi)):
            h_ref[at * rows : (at + 1) * rows, :] = y
        for j in range(0, n, BL):
            hi, lo = split(x[:, j : j + BL].T)
            for at, y in enumerate((hi, hi, lo)):
                t_ref[j : j + BL, at * rows : (at + 1) * rows] = y

    mask = (code_ref[0:1, :] == 2 * g + rel).astype(f32).astype(bf16)
    mask = jnp.concatenate([mask] * 3, axis=1)
    place = {b: p for p, b in enumerate(order)}
    for j in range(0, n, 2 * BL):
        prod = dot_nn(t_ref[j:n, :] * mask, h_ref[:, j : j + 2 * BL])
        for i in range(j, n, BL):
            for c in (j, j + BL):
                if i >= c:
                    p = place[(i // BL, c // BL)]
                    dst, p = (a_ref, p) if p < half else (b_ref, p - half)
                    dst[0, p * BL : (p + 1) * BL, :] = prod[i - j : i - j + BL, c - j : c - j + BL]


def gram(vec, code, table, n_group, rel):
    rows, n = vec.shape
    size = len(blocks(n)) * BL // 2
    return pl.pallas_call(
        lambda *refs: gram_body(rel, *refs),
        grid=(n_group,),
        in_specs=[
            pl.BlockSpec((rows, n), lambda g: (0, 0)),
            pl.BlockSpec(code.shape, lambda g: (0, 0)),
            pl.BlockSpec(table.shape, lambda g: (0, 0)),
        ],
        out_specs=[pl.BlockSpec((1, size, BL), lambda g: (g, 0, 0))] * 2,
        out_shape=[jax.ShapeDtypeStruct((n_group, size, BL), f32)] * 2,
        scratch_shapes=[
            pltpu.VMEM((n, 3 * rows), bf16),
            pltpu.VMEM((3 * rows, n), bf16),
        ],
        cost_estimate=pl.CostEstimate(
            flops=3 * n_group * rows * n * n, bytes_accessed=4 * (rows * n + 2 * n_group * size * BL), transcendentals=0
        ),
        name="gram",
    )(vec, code, table)


def diag_group(b, c, tt, s):
    lane = lax.broadcasted_iota(jnp.int32, (SUB, BL), 1)
    sub = lax.broadcasted_iota(jnp.int32, (SUB, BL), 0)
    base = SUB * s

    def columns(x):
        return [jnp.broadcast_to(x[:, base + u : base + u + 1], (SUB, BL)) for u in range(SUB)]

    for u, x in enumerate(columns(b[base : base + SUB, :])):
        c[SUB * u : SUB * u + SUB, :] = x
    rows = [jnp.broadcast_to(b[base + t : base + t + 1, :], (SUB, BL)) for t in range(SUB)]
    schur = {}
    for i in range(SUB):
        for u in range(i + 1):
            schur[i, u] = jnp.broadcast_to(c[SUB * u + i : SUB * u + i + 1, :], (SUB, BL))
    panel = (lane >= base) & (lane < base + SUB)
    fwd = [jnp.where(panel, jnp.where(lane == base + t, 1.0, 0.0), rows[t]) for t in range(SUB)]
    pivot, inv, mult = [], [], {}
    for t in range(SUB):
        pivot.append(schur[t, t])
        inv.append(1.0 / schur[t, t])
        for i in range(t + 1, SUB):
            mult[i, t] = schur[i, t] * inv[t]
        for u in range(t + 1, SUB):
            for i in range(u, SUB):
                schur[i, u] = schur[i, u] - mult[u, t] * schur[i, t]
        for i in range(t + 1, SUB):
            fwd[i] = fwd[i] - mult[i, t] * fwd[t]
    back = [None] * SUB
    for t in reversed(range(SUB)):
        w = fwd[t] * inv[t]
        for i in range(SUB - 1, t, -1):
            w = w - mult[i, t] * back[i]
        back[t] = w
    first = s - s % NEST
    for g in [*range(s + 1, first + NEST), *range(first, s)]:
        x = b[SUB * g : SUB * g + SUB, :]
        even, odd = 0.0, 0.0
        col = columns(x)
        for u in range(0, SUB, 2):
            even = even + col[u] * back[u]
            odd = odd + col[u + 1] * back[u + 1]
        b[SUB * g : SUB * g + SUB, :] = jnp.where(panel, 0.0, x) - (even + odd)
    out = jnp.zeros((SUB, BL), f32)
    full = jnp.zeros((SUB, BL), f32)
    for t in range(SUB):
        row = jnp.where(lane <= base + t, fwd[t] * lax.rsqrt(pivot[t]), 0.0)
        out = jnp.where(sub == t, row, out)
        full = jnp.where(sub == t, back[t], full)
    b[base : base + SUB, :] = full
    tt[base : base + SUB, :] = out


def diag_block(b, c, tt):
    wide = SUB * NEST
    lane = lax.broadcasted_iota(jnp.int32, (BL, BL), 1)
    for first in range(0, BL // SUB, NEST):
        for s in range(first, first + NEST):
            diag_group(b, c.at[s % 4], tt, s)
        low, high = SUB * first, SUB * first + wide
        if high < BL:
            w = b[low:high, :]
            pad = [jnp.zeros((low, BL), f32)] * (low > 0) + [w] + [jnp.zeros((BL - high, BL), f32)]
            wh, wl = split(jnp.concatenate(pad, axis=0))
            x = b[high:BL, :]
            xh, xl = split(x)
            inside = (lane[high:BL] >= low) & (lane[high:BL] < high)
            prod = dot_nn(
                jnp.concatenate([xh, xh, xl, xl], axis=1), jnp.concatenate([wh, wl, wh, wl], axis=0)
            )
            b[high:BL, :] = jnp.where(inside, 0.0, x) - prod


def chol_body(n, scale_ref, pa_ref, pb_ref, out_ref, w_ref, b_ref, c_ref, t_ref, h1_ref, h2_ref):
    nb = n // BL
    order = blocks(n)
    place = {b: p for p, b in enumerate(order)}
    half = len(order) // 2
    scale = scale_ref[0]
    row = lax.broadcasted_iota(jnp.int32, (BL, BL), 0)
    col = lax.broadcasted_iota(jnp.int32, (BL, BL), 1)
    for p, (i, j) in enumerate(order):
        src, q = (pa_ref, p) if p < half else (pb_ref, p - half)
        x = src[q * BL : (q + 1) * BL, :] * scale
        if i == j:
            x = x + jnp.where(row == col, ridge, 0.0)
        w_ref[i * BL : (i + 1) * BL, j * BL : (j + 1) * BL] = x

    @pl.loop(0, nb)
    def _(k):
        o = pl.multiple_of(k * BL, BL)
        b_ref[...] = w_ref[pl.ds(o, BL), pl.ds(o, BL)]
        diag_block(b_ref, c_ref, t_ref)
        out_ref[pl.ds(pl.multiple_of((len(order) + k) * BL, BL), BL), :] = t_ref[...]
        for kk in range(nb):

            @pl.when(k == kk)
            def _():
                c = kk * BL
                if kk % 2:
                    p = place[(kk, kk - 1)] * BL
                    q = (len(order) + kk - 1) * BL
                    x = dot3(out_ref[p : p + BL, :], out_ref[q : q + BL, :])
                    q = (len(order) + nb + kk // 2) * BL
                    out_ref[q : q + BL, :] = -dot3(t_ref[...], x)
                th, tl = split(t_ref[...])
                tcat = jnp.concatenate([th, tl, th, tl], axis=1)
                for i in range(c, n, BL):
                    ah, al = split(w_ref[i : i + BL, c : c + BL])
                    x = dot_nt(jnp.concatenate([ah, ah, al, al], axis=1), tcat)
                    if i == c:
                        x = jnp.where(row >= col, x, 0.0)
                    p = place[(i // BL, kk)]
                    out_ref[p * BL : (p + 1) * BL, :] = x
                    if i > c:
                        xh, xl = split(x)
                        h1_ref[i : i + BL, :] = jnp.concatenate([xh, xh, xl, xl], axis=1)
                        h2_ref[i : i + BL, :] = jnp.concatenate([xh, xl, xh, xl], axis=1)
                j = c + BL
                while j < n:
                    wide = BL if (j // BL) % 2 == 1 else 2 * BL
                    w_ref[j:n, j : j + wide] = w_ref[j:n, j : j + wide] - dot_nt(
                        h1_ref[j:n, :], h2_ref[j : j + wide, :]
                    )
                    j += wide


def chol(pa, pb, scale, n):
    size = len(blocks(n)) * BL
    return pl.pallas_call(
        lambda *refs: chol_body(n, *refs),
        in_specs=[
            pl.BlockSpec(memory_space=pltpu.SMEM),
            pl.BlockSpec(memory_space=pltpu.VMEM),
            pl.BlockSpec(memory_space=pltpu.VMEM),
        ],
        out_specs=pl.BlockSpec(memory_space=pltpu.VMEM),
        out_shape=jax.ShapeDtypeStruct((size + n + n // 2, BL), f32),
        scratch_shapes=[
            pltpu.VMEM((n, n), f32),
            pltpu.VMEM((BL, BL), f32),
            pltpu.VMEM((4, SUB * SUB, BL), f32),
            pltpu.VMEM((BL, BL), f32),
            pltpu.VMEM((n, 4 * BL), bf16),
            pltpu.VMEM((n, 4 * BL), bf16),
        ],
        cost_estimate=pl.CostEstimate(flops=40 * n * n * n, bytes_accessed=8 * size * BL, transcendentals=0),
        name="chol",
    )(scale, pa, pb)


def whiten_body(n, chunks, *refs):
    mine_ref, cent_ref, info_ref, own_hbm, other_hbm = refs[:5]
    res_hbm = refs[5 : 5 + chunks]
    out_ref, fac_ref, p_ref, r_ref, z_ref, o_ref, l_ref, t_ref, w_ref, sem = refs[5 + chunks :]
    order = blocks(n)
    place = {b: p for p, b in enumerate(order)}
    nb = n // BL
    wide = 2 * BL
    mine = mine_ref[0]
    _, sources, part, _ = r_ref.shape
    rows = sources * part
    used = [0]

    def copy(src, dst):
        one = pltpu.make_async_copy(src, dst, sem.at[used[0]])
        used[0] += 1
        one.start()
        return one

    packs = [copy(own_hbm, p_ref.at[0])]
    moved = [copy(res_hbm[q], r_ref.at[q]) for q in range(chunks)]
    packs.append(copy(other_hbm, p_ref.at[1]))
    z_ref[...] = jnp.zeros_like(z_ref)

    low = part.bit_length() - 1
    row = lax.broadcasted_iota(jnp.int32, (rows, sources), 0)
    pick = ((row >> low) == lax.broadcasted_iota(jnp.int32, (rows, sources), 1)).astype(f32).astype(bf16)
    spread = dot_nn(pick, info_ref[...].astype(f32).astype(bf16))
    k = lax.broadcasted_iota(jnp.int32, (rows, BL), 0) & (part - 1)
    lane = lax.broadcasted_iota(jnp.int32, (rows, BL), 1)
    tags = [jnp.sum(jnp.where(lane == k + q * part, spread, 0.0), axis=1, keepdims=True) for q in range(chunks)]

    done = []
    for slot, dst in enumerate((mine, 1 - mine)):
        packs[slot].wait()
        for j in range(nb):
            p = place[(j, j)] * BL
            done.append(
                copy(
                    p_ref.at[slot, pl.ds(p, n - j * BL), :],
                    fac_ref.at[dst, pl.ds(j * BL, n - j * BL), pl.ds(j * BL, BL)],
                )
            )
            if j + 1 < nb:
                rest = n - (j + 1) * BL
                done.append(
                    copy(
                        z_ref.at[:, pl.ds(0, rest)],
                        fac_ref.at[dst, pl.ds(j * BL, BL), pl.ds((j + 1) * BL, rest)],
                    )
                )
        for p, (i, j) in enumerate(order):
            if i // 2 == j // 2:
                continue
            hi, lo = split(p_ref[slot, p * BL : (p + 1) * BL, :])
            c = (j // 2) * 3 * wide + (j % 2) * BL
            for at, x in enumerate((hi, hi, lo)):
                l_ref[slot, i * BL : (i + 1) * BL, c + at * wide : c + at * wide + BL] = x
        for k in range(nb):
            p = (len(order) + k) * BL
            c = (k % 2) * BL
            hi, lo = split(p_ref[slot, p : p + BL, :])
            if k % 2:
                p = (len(order) + nb + k // 2) * BL
                hi2, lo2 = split(p_ref[slot, p : p + BL, :])
            else:
                hi2 = lo2 = jnp.zeros((BL, BL), bf16)
            for at, (x, y) in enumerate(((hi, hi2), (hi, hi2), (lo, lo2))):
                t_ref[slot, k * BL : (k + 1) * BL, at * wide + c : at * wide + c + BL] = x
                t_ref[slot, k * BL : (k + 1) * BL, at * wide + BL - c : at * wide + wide - c] = y

    for one in moved:
        one.wait()
    for c in range(0, n, wide):
        for slot in range(2):
            which = mine if slot == 0 else 1 - mine
            prod = None
            if c:
                prod = dot_nt(w_ref[slot, :, : 3 * c], l_ref[slot, c : c + wide, : 3 * c])
            accs = []
            for q in range(chunks):
                x = r_ref[q, :, :, c : c + wide].reshape(rows, wide)
                x = jnp.where(tags[q] == (which + 1).astype(f32), x - cent_ref[pl.ds(which, 1), c : c + wide], 0.0)
                if prod is not None:
                    x = x - prod[q * rows : (q + 1) * rows]
                accs.append(x)
            ah, al = split(jnp.concatenate(accs, axis=0) if chunks > 1 else accs[0])
            x = dot_nt(jnp.concatenate([ah, al, ah], axis=1), t_ref[slot, c : c + wide, :])
            if c + wide < n:
                hi, lo = split(x)
                for at, y in enumerate((hi, lo, hi)):
                    w_ref[slot, :, 3 * c + at * wide : 3 * c + (at + 1) * wide] = y
            for q in range(chunks):
                y = x[q * rows : (q + 1) * rows].reshape(sources, part, wide)
                if slot:
                    y = y + o_ref[q, :, :, c : c + wide]
                o_ref[q, :, :, c : c + wide] = y
        for q in range(chunks):
            done.append(
                copy(
                    o_ref.at[q, :, :, pl.ds(c, wide)],
                    out_ref.at[:, pl.ds(q * part, part), pl.ds(c, wide)],
                )
            )
    for one in done:
        one.wait()


def whiten(res, info, own, other, mine, centroids):
    chunks = len(res)
    sources, part, n = res[0].shape
    rows = chunks * sources * part
    nb = n // BL
    vmem = pl.BlockSpec(memory_space=pltpu.VMEM)
    hbm = pl.BlockSpec(memory_space=pltpu.HBM)
    return pl.pallas_call(
        lambda *refs: whiten_body(n, chunks, *refs),
        in_specs=[pl.BlockSpec(memory_space=pltpu.SMEM), vmem, vmem] + [hbm] * (2 + chunks),
        out_specs=[hbm, hbm],
        out_shape=[
            jax.ShapeDtypeStruct((sources, chunks * part, n), f32),
            jax.ShapeDtypeStruct((2, n, n), f32),
        ],
        scratch_shapes=[
            pltpu.VMEM((2,) + own.shape, f32),
            pltpu.VMEM((chunks, sources, part, n), f32),
            pltpu.VMEM((BL, n - BL), f32),
            pltpu.VMEM((chunks, sources, part, n), f32),
            pltpu.VMEM((2, n, 3 * (n - 2 * BL)), bf16),
            pltpu.VMEM((2, n, 6 * BL), bf16),
            pltpu.VMEM((2, rows, 3 * (n - 2 * BL)), bf16),
            pltpu.SemaphoreType.DMA((2 + chunks + 2 * (2 * nb - 1) + chunks * (nb // 2),)),
        ],
        cost_estimate=pl.CostEstimate(flops=12 * rows * n * n, bytes_accessed=16 * n * n, transcendentals=0),
        name="whiten",
    )(mine, centroids, info, own, other, *res)


def flip(x, axis, bit):
    size = lax.axis_size(axis)
    return lax.ppermute(x, axis, [(i, i ^ (1 << bit)) for i in range(size)])


def bit_of(axis, bit):
    return (lax.axis_index(axis) >> bit) & 1


def halve(terms, axis, bit, dim):
    b = bit_of(axis, bit)
    got = flip(sum(lax.dynamic_slice_in_dim(x, 1 - b, 1, dim) for x in terms), axis, bit)
    return (sum(lax.dynamic_slice_in_dim(x, b, 1, dim) for x in terms) + got,)


def double(x, axis, bit, dim):
    got = flip(x, axis, bit)
    low = bit_of(axis, bit) == 0
    return jnp.where(low, jnp.concatenate([x, got], dim), jnp.concatenate([got, x], dim))


def sum_and_share(parts, n_group, n_member, before_last):
    gbits = n_group.bit_length() - 1
    mbits = n_member.bit_length() - 1
    rows = parts[0][0].shape[1]
    shape = (2,) * gbits + (2,) * (mbits - 1)
    ghalf = [("group", b, gbits - 1 - b) for b in range(gbits)]
    mhalf = [("member", b, gbits + b - 1) for b in range(1, mbits)]
    plans = [ghalf + mhalf, mhalf[:1] + ghalf + mhalf[1:]]
    gathers = [mhalf[::-1], mhalf[:1] + mhalf[:0:-1]]
    parts = [tuple(x.reshape(shape + (rows >> (mbits - 1), BL)) for x in terms) for terms in parts]
    for step in range(gbits + mbits - 1):
        parts = [halve(parts[c], *plans[c][step]) for c in range(2)]
    parts = [sum(terms) for terms in parts]
    for step in range(mbits - 1):
        if step == mbits - 2:
            parts = before_last(parts)
        parts = [double(parts[c], *gathers[c][step]) for c in range(2)]
    return [p.reshape(rows, BL) for p in parts]


def to_owners(x):
    return lax.all_to_all(x, ("group", "member"), split_axis=0, concat_axis=0, tiled=True)


def on_device(rows, old_list, old_centroids, dest_device, new_local, centroids):
    n_group = lax.axis_size("group")
    n_member = lax.axis_size("member")
    devices = n_group * n_member
    row_dev, width = rows.shape
    lists = centroids.shape[0]
    capacity = max(2, 2 * row_dev // devices)
    group = lax.axis_index("group")
    core = lax.axis_index("member") & 1

    seen = [centroids]
    for shift in range(1, n_group):
        seen.append(lax.ppermute(centroids, "group", [(i, (i + shift) % n_group) for i in range(n_group)]))
    spare = -(n_group * lists) % SUB
    seen = jnp.concatenate(seen + [jnp.zeros((spare, width), f32)] * (spare > 0), axis=0)

    chunk = capacity // 2 if capacity % (2 * SUB) == 0 else capacity
    *outgoing, vectors, info, code = route(
        jnp.stack([group, core]),
        rows,
        old_list.reshape(1, -1),
        dest_device.reshape(1, -1),
        new_local.reshape(1, -1),
        old_centroids,
        (n_group, n_member, capacity, chunk),
    )
    outgoing = [x.reshape(devices, chunk, width) for x in outgoing]

    first = to_owners(outgoing[0])
    away = gram(vectors, code, seen, n_group, 1)
    kept = gram(vectors, code, seen, n_group, 0)
    parts = [(k, flip(x, "member", 0)) for k, x in zip(kept, away)]
    info, first = lax.optimization_barrier((info.reshape(devices, 1, BL), first))
    info = to_owners(info)[:, 0]
    counts = jnp.sum(info[:, capacity : capacity + lists], axis=0).astype(f32)
    count = lax.dynamic_index_in_dim(counts, core, 0, keepdims=True)
    scale = 1.0 / jnp.maximum(count, 1.0)
    arrived = [first]

    def before_last(parts):
        nonlocal scale
        for later in outgoing[1:]:
            later, scale, *parts = lax.optimization_barrier((later, scale, *parts))
            arrived.append(to_owners(later))
        return parts

    pa, pb = sum_and_share(parts, n_group, n_member, before_last)
    own = chol(pa, pb, scale, width)
    other = flip(own, "member", 0)
    result, factors = whiten(arrived, info, own, other, core.reshape(1), centroids)
    return (result.reshape(devices * capacity, width), factors)


def solution(mesh):
    return jax.shard_map(
        on_device,
        mesh=mesh,
        in_specs=(
            P(("group", "member"), None),
            P(("group", "member")),
            P(),
            P(("group", "member"), None),
            P(("group", "member")),
            P("group", None),
        ),
        out_specs=(P(("group", "member"), None), P("group", None, None)),
        check_vma=False,
    )
```

```python
import jax
import jax.numpy as jnp
from jax import lax
from jax.experimental import pallas as pl
from jax.experimental.pallas import tpu as pltpu
from jax.sharding import PartitionSpec as P


ridge = 0.1
f32 = jnp.float32
bf16 = jnp.bfloat16
BL = 128
SUB = 8
NEST = 8


def split(x):
    hi = x.astype(bf16)
    return hi, (x - hi.astype(f32)).astype(bf16)


def dot_nt(a, b):
    return lax.dot_general(a, b, (((1,), (1,)), ((), ())), preferred_element_type=f32)


def dot_nn(a, b):
    return lax.dot_general(a, b, (((1,), (0,)), ((), ())), preferred_element_type=f32)


def dot3(a, b):
    ah, al = split(a)
    bh, bl = split(b)
    return dot_nn(ah, bh) + (dot_nn(ah, bl) + dot_nn(al, bh))


def blocks(n):
    nb = n // BL
    return [(i, j) for j in range(nb) for i in range(j, nb)]


def split3(x):
    hi = x.astype(bf16)
    rest = x - hi.astype(f32)
    mid = rest.astype(bf16)
    return hi, mid, (rest - mid.astype(f32)).astype(bf16)


def table_rows(index, table):
    count = table.shape[0]
    hot = (lax.broadcasted_iota(jnp.int32, (count, index.shape[1]), 0) == index).astype(f32)
    hot = jnp.concatenate([hot] * 3, axis=0).astype(bf16)
    return lax.dot_general(
        hot, jnp.concatenate(split3(table), axis=0), (((0,), (0,)), ((), ())), preferred_element_type=f32
    )


def route_body(sizes, ids_ref, rows_hbm, old_ref, dest_ref, local_ref, table_hbm, *refs):
    n_group, n_member, capacity, chunk = sizes
    devices = n_group * n_member
    chunks = capacity // chunk
    out_refs = refs[:chunks]
    vec_hbm, info_ref, code_ref, rows_ref, table_ref, vec_ref, o_ref, sem = refs[chunks:]
    count, _ = rows_ref.shape
    loads = [
        pltpu.make_async_copy(rows_hbm, rows_ref, sem.at[0]),
        pltpu.make_async_copy(table_hbm, table_ref, sem.at[1]),
    ]
    for copy in loads:
        copy.start()
    group, core = ids_ref[0], ids_ref[1]
    dest = dest_ref[...]
    local = local_ref[...]
    shift = n_member.bit_length() - 1
    device = lax.broadcasted_iota(jnp.int32, (devices, count), 0)
    onehot = (device == dest).astype(f32)
    earlier = lax.broadcasted_iota(jnp.int32, (count, count), 0) < lax.broadcasted_iota(jnp.int32, (count, count), 1)
    ahead = dot_nn(onehot.astype(bf16), earlier.astype(f32).astype(bf16))
    rank = jnp.sum(onehot * ahead, axis=0, keepdims=True).astype(jnp.int32)
    low = chunk.bit_length() - 1
    place = (rank >> low) * (devices * chunk) + dest * chunk + (rank & (chunk - 1))

    to_group = dest >> shift
    row = lax.broadcasted_iota(jnp.int32, (SUB, count), 0)
    code = to_group * 2 + (local ^ core)
    seen = ((group - to_group) & (n_group - 1)) * 2 + local
    code_ref[...] = jnp.where(row == 0, code, seen)

    slot = lax.broadcasted_iota(jnp.int32, (BL, count), 0)
    left = jnp.concatenate(
        [onehot * (local + 1).astype(f32), ((device >> shift) == to_group).astype(f32)], axis=1
    )
    right = jnp.concatenate(
        [((slot == rank) & (slot < capacity)).astype(f32), ((slot - capacity) == local).astype(f32)], axis=1
    )
    info_ref[...] = dot_nt(left.astype(bf16), right.astype(bf16)).astype(jnp.int32)

    for copy in loads:
        copy.wait()
    vec = rows_ref[...] + table_rows(old_ref[...], table_ref[...])
    vec_ref[...] = vec
    hi, mid, lo = split3(vec)
    copies = []
    for q in range(chunks):
        for r in range(0, devices * chunk, 2 * BL):
            base = q * devices * chunk + r
            pick = (lax.broadcasted_iota(jnp.int32, (2 * BL, count), 0) + base == place).astype(f32).astype(bf16)
            o_ref[base : base + 2 * BL, :] = dot_nn(pick, hi) + (dot_nn(pick, mid) + dot_nn(pick, lo))
            copies.append(
                pltpu.make_async_copy(
                    o_ref.at[pl.ds(base, 2 * BL), :], out_refs[q].at[pl.ds(r, 2 * BL), :], sem.at[3 + base // (2 * BL)]
                )
            )
            copies[-1].start()
    copies.append(pltpu.make_async_copy(vec_ref, vec_hbm, sem.at[2]))
    copies[-1].start()
    for copy in copies:
        copy.wait()


def route(ids, rows, old, dest, local, table, sizes):
    n_group, n_member, capacity, chunk = sizes
    devices = n_group * n_member
    count, n = rows.shape
    chunks = capacity // chunk
    vmem = pl.BlockSpec(memory_space=pltpu.VMEM)
    hbm = pl.BlockSpec(memory_space=pltpu.HBM)
    return pl.pallas_call(
        lambda *refs: route_body(sizes, *refs),
        in_specs=[pl.BlockSpec(memory_space=pltpu.SMEM), hbm, vmem, vmem, vmem, hbm],
        out_specs=[hbm] * (chunks + 1) + [vmem] * 2,
        out_shape=[jax.ShapeDtypeStruct((devices * chunk, n), f32)] * chunks
        + [
            jax.ShapeDtypeStruct((count, n), f32),
            jax.ShapeDtypeStruct((devices, BL), jnp.int32),
            jax.ShapeDtypeStruct((SUB, count), jnp.int32),
        ],
        scratch_shapes=[
            pltpu.VMEM((count, n), f32),
            pltpu.VMEM(table.shape, f32),
            pltpu.VMEM((count, n), f32),
            pltpu.VMEM((devices * capacity, n), f32),
            pltpu.SemaphoreType.DMA((3 + devices * capacity // (2 * BL),)),
        ],
        cost_estimate=pl.CostEstimate(
            flops=6 * devices * capacity * count * n, bytes_accessed=4 * devices * capacity * n, transcendentals=0
        ),
        name="route",
    )(ids, rows, old, dest, local, table)


def gram_body(rel, vec_ref, code_ref, table_ref, a_ref, b_ref, t_ref, h_ref):
    g = pl.program_id(0)
    rows, n = vec_ref.shape
    order = blocks(n)
    half = len(order) // 2

    @pl.when(g == 0)
    def _():
        x = vec_ref[...] - table_rows(code_ref[1:2, :], table_ref[...])
        hi, lo = split(x)
        for at, y in enumerate((hi, lo, hi)):
            h_ref[at * rows : (at + 1) * rows, :] = y
        for j in range(0, n, BL):
            hi, lo = split(x[:, j : j + BL].T)
            for at, y in enumerate((hi, hi, lo)):
                t_ref[j : j + BL, at * rows : (at + 1) * rows] = y

    mask = (code_ref[0:1, :] == 2 * g + rel).astype(f32).astype(bf16)
    mask = jnp.concatenate([mask] * 3, axis=1)
    place = {b: p for p, b in enumerate(order)}
    for j in range(0, n, 2 * BL):
        prod = dot_nn(t_ref[j:n, :] * mask, h_ref[:, j : j + 2 * BL])
        for i in range(j, n, BL):
            for c in (j, j + BL):
                if i >= c:
                    p = place[(i // BL, c // BL)]
                    dst, p = (a_ref, p) if p < half else (b_ref, p - half)
                    dst[0, p * BL : (p + 1) * BL, :] = prod[i - j : i - j + BL, c - j : c - j + BL]


def gram(vec, code, table, n_group, rel):
    rows, n = vec.shape
    size = len(blocks(n)) * BL // 2
    return pl.pallas_call(
        lambda *refs: gram_body(rel, *refs),
        grid=(n_group,),
        in_specs=[
            pl.BlockSpec((rows, n), lambda g: (0, 0)),
            pl.BlockSpec(code.shape, lambda g: (0, 0)),
            pl.BlockSpec(table.shape, lambda g: (0, 0)),
        ],
        out_specs=[pl.BlockSpec((1, size, BL), lambda g: (g, 0, 0))] * 2,
        out_shape=[jax.ShapeDtypeStruct((n_group, size, BL), f32)] * 2,
        scratch_shapes=[
            pltpu.VMEM((n, 3 * rows), bf16),
            pltpu.VMEM((3 * rows, n), bf16),
        ],
        compiler_params=pltpu.CompilerParams(vmem_limit_bytes=24 << 20),
        cost_estimate=pl.CostEstimate(
            flops=3 * n_group * rows * n * n, bytes_accessed=4 * (rows * n + 2 * n_group * size * BL), transcendentals=0
        ),
        name="gram",
    )(vec, code, table)


def diag_group(b, c, tt, s):
    lane = lax.broadcasted_iota(jnp.int32, (SUB, BL), 1)
    sub = lax.broadcasted_iota(jnp.int32, (SUB, BL), 0)
    base = SUB * s

    def columns(x):
        return [jnp.broadcast_to(x[:, base + u : base + u + 1], (SUB, BL)) for u in range(SUB)]

    for u, x in enumerate(columns(b[base : base + SUB, :])):
        c[SUB * u : SUB * u + SUB, :] = x
    rows = [jnp.broadcast_to(b[base + t : base + t + 1, :], (SUB, BL)) for t in range(SUB)]
    schur = {}
    for i in range(SUB):
        for u in range(i + 1):
            schur[i, u] = jnp.broadcast_to(c[SUB * u + i : SUB * u + i + 1, :], (SUB, BL))
    panel = (lane >= base) & (lane < base + SUB)
    fwd = [jnp.where(panel, jnp.where(lane == base + t, 1.0, 0.0), rows[t]) for t in range(SUB)]
    pivot, inv, mult = [], [], {}
    for t in range(SUB):
        pivot.append(schur[t, t])
        inv.append(1.0 / schur[t, t])
        for i in range(t + 1, SUB):
            mult[i, t] = schur[i, t] * inv[t]
        for u in range(t + 1, SUB):
            for i in range(u, SUB):
                schur[i, u] = schur[i, u] - mult[u, t] * schur[i, t]
        for i in range(t + 1, SUB):
            fwd[i] = fwd[i] - mult[i, t] * fwd[t]
    back = [None] * SUB
    for t in reversed(range(SUB)):
        w = fwd[t] * inv[t]
        for i in range(SUB - 1, t, -1):
            w = w - mult[i, t] * back[i]
        back[t] = w
    first = s - s % NEST
    for g in [*range(s + 1, first + NEST), *range(first, s)]:
        x = b[SUB * g : SUB * g + SUB, :]
        even, odd = 0.0, 0.0
        col = columns(x)
        for u in range(0, SUB, 2):
            even = even + col[u] * back[u]
            odd = odd + col[u + 1] * back[u + 1]
        b[SUB * g : SUB * g + SUB, :] = jnp.where(panel, 0.0, x) - (even + odd)
    out = jnp.zeros((SUB, BL), f32)
    full = jnp.zeros((SUB, BL), f32)
    for t in range(SUB):
        row = jnp.where(lane <= base + t, fwd[t] * lax.rsqrt(pivot[t]), 0.0)
        out = jnp.where(sub == t, row, out)
        full = jnp.where(sub == t, back[t], full)
    b[base : base + SUB, :] = full
    tt[base : base + SUB, :] = out


def diag_block(b, c, tt):
    wide = SUB * NEST
    lane = lax.broadcasted_iota(jnp.int32, (BL, BL), 1)
    for first in range(0, BL // SUB, NEST):
        for s in range(first, first + NEST):
            diag_group(b, c.at[s % 4], tt, s)
        low, high = SUB * first, SUB * first + wide
        if high < BL:
            w = b[low:high, :]
            pad = [jnp.zeros((low, BL), f32)] * (low > 0) + [w] + [jnp.zeros((BL - high, BL), f32)]
            wh, wl = split(jnp.concatenate(pad, axis=0))
            x = b[high:BL, :]
            xh, xl = split(x)
            inside = (lane[high:BL] >= low) & (lane[high:BL] < high)
            prod = dot_nn(
                jnp.concatenate([xh, xh, xl, xl], axis=1), jnp.concatenate([wh, wl, wh, wl], axis=0)
            )
            b[high:BL, :] = jnp.where(inside, 0.0, x) - prod


def chol_body(n, scale_ref, pa_ref, pb_ref, out_ref, w_ref, b_ref, c_ref, t_ref, h1_ref, h2_ref):
    nb = n // BL
    order = blocks(n)
    place = {b: p for p, b in enumerate(order)}
    half = len(order) // 2
    scale = scale_ref[0]
    row = lax.broadcasted_iota(jnp.int32, (BL, BL), 0)
    col = lax.broadcasted_iota(jnp.int32, (BL, BL), 1)
    for p, (i, j) in enumerate(order):
        src, q = (pa_ref, p) if p < half else (pb_ref, p - half)
        x = src[q * BL : (q + 1) * BL, :] * scale
        if i == j:
            x = x + jnp.where(row == col, ridge, 0.0)
        w_ref[i * BL : (i + 1) * BL, j * BL : (j + 1) * BL] = x

    @pl.loop(0, nb)
    def _(k):
        o = pl.multiple_of(k * BL, BL)
        b_ref[...] = w_ref[pl.ds(o, BL), pl.ds(o, BL)]
        diag_block(b_ref, c_ref, t_ref)
        out_ref[pl.ds(pl.multiple_of((len(order) + k) * BL, BL), BL), :] = t_ref[...]
        for kk in range(nb):

            @pl.when(k == kk)
            def _():
                c = kk * BL
                if kk % 2:
                    p = place[(kk, kk - 1)] * BL
                    q = (len(order) + kk - 1) * BL
                    x = dot3(out_ref[p : p + BL, :], out_ref[q : q + BL, :])
                    q = (len(order) + nb + kk // 2) * BL
                    out_ref[q : q + BL, :] = -dot3(t_ref[...], x)
                th, tl = split(t_ref[...])
                tcat = jnp.concatenate([th, tl, th, tl], axis=1)
                ah, al = split(w_ref[c:n, c : c + BL])
                x = dot_nt(jnp.concatenate([ah, ah, al, al], axis=1), tcat)
                p = place[(kk, kk)] * BL
                out_ref[p : p + BL, :] = jnp.where(row >= col, x[:BL], 0.0)
                if kk + 1 < nb:
                    x = x[BL:]
                    out_ref[p + BL : p + n - c, :] = x
                    xh, xl = split(x)
                    h1_ref[c + BL : n, :] = jnp.concatenate([xh, xh, xl, xl], axis=1)
                    h2_ref[c + BL : n, :] = jnp.concatenate([xh, xl, xh, xl], axis=1)
                j = c + BL
                while j < n:
                    wide = BL if (j // BL) % 2 == 1 else 2 * BL
                    w_ref[j:n, j : j + wide] = w_ref[j:n, j : j + wide] - dot_nt(
                        h1_ref[j:n, :], h2_ref[j : j + wide, :]
                    )
                    j += wide


def chol(pa, pb, scale, n):
    size = len(blocks(n)) * BL
    return pl.pallas_call(
        lambda *refs: chol_body(n, *refs),
        in_specs=[
            pl.BlockSpec(memory_space=pltpu.SMEM),
            pl.BlockSpec(memory_space=pltpu.VMEM),
            pl.BlockSpec(memory_space=pltpu.VMEM),
        ],
        out_specs=pl.BlockSpec(memory_space=pltpu.VMEM),
        out_shape=jax.ShapeDtypeStruct((size + n + n // 2, BL), f32),
        scratch_shapes=[
            pltpu.VMEM((n, n), f32),
            pltpu.VMEM((BL, BL), f32),
            pltpu.VMEM((4, SUB * SUB, BL), f32),
            pltpu.VMEM((BL, BL), f32),
            pltpu.VMEM((n, 4 * BL), bf16),
            pltpu.VMEM((n, 4 * BL), bf16),
        ],
        cost_estimate=pl.CostEstimate(flops=40 * n * n * n, bytes_accessed=8 * size * BL, transcendentals=0),
        name="chol",
    )(scale, pa, pb)


def tall(x):
    hi, lo = split(x)
    return jnp.concatenate([hi, hi, lo], axis=0)


def flat(x):
    hi, lo = split(x)
    return jnp.concatenate([hi, lo, hi], axis=1)


def invert_body(n, p_ref, out_ref, l_ref, x_ref):
    order = blocks(n)
    nb = n // BL
    wide = 2 * BL
    for p, (i, j) in enumerate(order):
        if i // 2 != j // 2:
            l_ref[i * BL : (i + 1) * BL, j * BL : (j + 1) * BL] = p_ref[p * BL : (p + 1) * BL, :]
    x_ref[...] = jnp.zeros_like(x_ref)
    for k in range(nb):
        o = k * BL
        p = (len(order) + k) * BL
        x_ref[o : o + BL, o : o + BL] = p_ref[p : p + BL, :]
        if k % 2:
            p = (len(order) + nb + k // 2) * BL
            x_ref[o : o + BL, o - BL : o] = p_ref[p : p + BL, :]
    size = wide
    while size < n:
        for o in range(0, n, 2 * size):
            m = o + size
            e = m + size
            y = dot_nn(flat(l_ref[m:e, o:m]), tall(x_ref[o:m, o:m]))
            x_ref[m:e, o:m] = -dot_nn(flat(x_ref[m:e, m:e]), tall(y))
        size *= 2
    at = 0
    for i in range(0, n, wide):
        for j in range(0, i + wide, wide):
            out_ref[at : at + wide, :] = x_ref[i : i + wide, j : j + wide]
            at += wide


def invert(pack, n):
    m = n // (2 * BL)
    size = m * (m + 1) // 2 * 2 * BL
    vmem = pl.BlockSpec(memory_space=pltpu.VMEM)
    return pl.pallas_call(
        lambda *refs: invert_body(n, *refs),
        in_specs=[vmem],
        out_specs=vmem,
        out_shape=jax.ShapeDtypeStruct((size, 2 * BL), f32),
        scratch_shapes=[pltpu.VMEM((n, n), f32), pltpu.VMEM((n, n), f32)],
        cost_estimate=pl.CostEstimate(flops=2 * n * n * n, bytes_accessed=4 * n * n, transcendentals=0),
        name="invert",
    )(pack)


def whiten_body(n, chunks, *refs):
    mine_ref, cent_ref, info_ref, own_hbm, other_hbm, own_inv, other_inv = refs[:7]
    res_hbm = refs[7 : 7 + chunks]
    out_ref, fac_ref, p_ref, x_ref, r_ref, z_ref, o_ref, a_ref, b_ref, sem = refs[7 + chunks :]
    order = blocks(n)
    place = {b: p for p, b in enumerate(order)}
    nb = n // BL
    wide = 2 * BL
    mine = mine_ref[0]
    _, sources, part, _ = r_ref.shape
    rows = sources * part
    used = [0]

    def copy(src, dst):
        one = pltpu.make_async_copy(src, dst, sem.at[used[0]])
        used[0] += 1
        one.start()
        return one

    moved = [copy(res_hbm[q], r_ref.at[q]) for q in range(chunks)]
    inverses = [copy(src, x_ref.at[slot]) for slot, src in enumerate((own_inv, other_inv))]
    size = len(order) * BL
    packs = [copy(src.at[pl.ds(0, size), :], p_ref.at[slot]) for slot, src in enumerate((own_hbm, other_hbm))]
    z_ref[...] = jnp.zeros_like(z_ref)

    low = part.bit_length() - 1
    row = lax.broadcasted_iota(jnp.int32, (rows, sources), 0)
    pick = ((row >> low) == lax.broadcasted_iota(jnp.int32, (rows, sources), 1)).astype(f32).astype(bf16)
    spread = dot_nn(pick, info_ref[...].astype(f32).astype(bf16))
    k = lax.broadcasted_iota(jnp.int32, (rows, BL), 0) & (part - 1)
    lane = lax.broadcasted_iota(jnp.int32, (rows, BL), 1)

    for q in range(chunks):
        moved[q].wait()
        tag = jnp.sum(jnp.where(lane == k + q * part, spread, 0.0), axis=1, keepdims=True)
        on = [tag == (which + 1).astype(f32) for which in (mine, 1 - mine)]
        for c in range(0, n, wide):
            x = r_ref[q, :, :, c : c + wide].reshape(rows, wide)
            x = x - jnp.where(on[0], cent_ref[pl.ds(mine, 1), c : c + wide], cent_ref[pl.ds(1 - mine, 1), c : c + wide])
            for slot in range(2):
                hi, lo = split(jnp.where(on[slot], x, 0.0))
                for at, y in enumerate((hi, lo, hi)):
                    a_ref[slot, q * rows : (q + 1) * rows, 3 * c + at * wide : 3 * c + (at + 1) * wide] = y
    for one in inverses:
        one.wait()
    done = []
    at = 0
    for c in range(0, n, wide):
        for slot in range(2):
            for j in range(0, c + wide, wide):
                hi, lo = split(x_ref[slot, at + j : at + j + wide, :])
                for t, y in enumerate((hi, hi, lo)):
                    b_ref[slot, c : c + wide, 3 * j + t * wide : 3 * j + (t + 1) * wide] = y
        at += c + wide
        x = sum(
            dot_nt(a_ref[slot, :, : 3 * (c + wide)], b_ref[slot, c : c + wide, : 3 * (c + wide)]) for slot in range(2)
        )
        for q in range(chunks):
            o_ref[q, :, :, c : c + wide] = x[q * rows : (q + 1) * rows].reshape(sources, part, wide)
            done.append(
                copy(
                    o_ref.at[q, :, :, pl.ds(c, wide)],
                    out_ref.at[:, pl.ds(q * part, part), pl.ds(c, wide)],
                )
            )
        if c == 0:
            for slot, dst in enumerate((mine, 1 - mine)):
                packs[slot].wait()
                for j in range(nb):
                    p = place[(j, j)] * BL
                    done.append(
                        copy(
                            p_ref.at[slot, pl.ds(p, n - j * BL), :],
                            fac_ref.at[dst, pl.ds(j * BL, n - j * BL), pl.ds(j * BL, BL)],
                        )
                    )
                    if j + 1 < nb:
                        rest = n - (j + 1) * BL
                        done.append(
                            copy(
                                z_ref.at[:, pl.ds(0, rest)],
                                fac_ref.at[dst, pl.ds(j * BL, BL), pl.ds((j + 1) * BL, rest)],
                            )
                        )
    for one in done:
        one.wait()


def whiten(res, info, own, other, own_inv, other_inv, mine, centroids):
    chunks = len(res)
    sources, part, n = res[0].shape
    rows = chunks * sources * part
    nb = n // BL
    vmem = pl.BlockSpec(memory_space=pltpu.VMEM)
    hbm = pl.BlockSpec(memory_space=pltpu.HBM)
    return pl.pallas_call(
        lambda *refs: whiten_body(n, chunks, *refs),
        in_specs=[pl.BlockSpec(memory_space=pltpu.SMEM), vmem, vmem]
        + [pl.BlockSpec(memory_space=pl.ANY)] * (4 + chunks),
        out_specs=[hbm, hbm],
        out_shape=[
            jax.ShapeDtypeStruct((sources, chunks * part, n), f32),
            jax.ShapeDtypeStruct((2, n, n), f32),
        ],
        scratch_shapes=[
            pltpu.VMEM((2, len(blocks(n)) * BL, BL), f32),
            pltpu.VMEM((2,) + own_inv.shape, f32),
            pltpu.VMEM((chunks, sources, part, n), f32),
            pltpu.VMEM((BL, n - BL), f32),
            pltpu.VMEM((chunks, sources, part, n), f32),
            pltpu.VMEM((2, rows, 3 * n), bf16),
            pltpu.VMEM((2, n, 3 * n), bf16),
            pltpu.SemaphoreType.DMA((4 + chunks + 2 * (2 * nb - 1) + chunks * (nb // 2),)),
        ],
        compiler_params=pltpu.CompilerParams(vmem_limit_bytes=50 << 20),
        cost_estimate=pl.CostEstimate(flops=12 * rows * n * n, bytes_accessed=16 * n * n, transcendentals=0),
        name="whiten",
    )(mine, centroids, info, own, other, own_inv, other_inv, *res)


def flip(x, axis, bit):
    size = lax.axis_size(axis)
    return lax.ppermute(x, axis, [(i, i ^ (1 << bit)) for i in range(size)])


def bit_of(axis, bit):
    return (lax.axis_index(axis) >> bit) & 1


def halve(terms, axis, bit, dim):
    b = bit_of(axis, bit)
    got = flip(sum(lax.dynamic_slice_in_dim(x, 1 - b, 1, dim) for x in terms), axis, bit)
    return (sum(lax.dynamic_slice_in_dim(x, b, 1, dim) for x in terms) + got,)


def double(x, axis, bit, dim):
    got = flip(x, axis, bit)
    low = bit_of(axis, bit) == 0
    return jnp.where(low, jnp.concatenate([x, got], dim), jnp.concatenate([got, x], dim))


def sum_and_share(parts, n_group, n_member):
    gbits = n_group.bit_length() - 1
    mbits = n_member.bit_length() - 1
    rows = parts[0][0].shape[1]
    shape = (2,) * gbits + (2,) * (mbits - 1)
    ghalf = [("group", b, gbits - 1 - b) for b in range(gbits)]
    mhalf = [("member", b, gbits + b - 1) for b in range(1, mbits)]
    plans = [ghalf + mhalf, mhalf[:1] + ghalf + mhalf[1:]]
    gathers = [mhalf[::-1], mhalf[:1] + mhalf[:0:-1]]
    parts = [tuple(x.reshape(shape + (rows >> (mbits - 1), BL)) for x in terms) for terms in parts]
    for step in range(gbits + mbits - 1):
        parts = [halve(parts[c], *plans[c][step]) for c in range(2)]
    parts = [sum(terms) for terms in parts]
    for step in range(mbits - 1):
        parts = [double(parts[c], *gathers[c][step]) for c in range(2)]
    return [p.reshape(rows, BL) for p in parts]


def to_owners(x):
    return lax.all_to_all(x, ("group", "member"), split_axis=0, concat_axis=0, tiled=True)


def on_device(rows, old_list, old_centroids, dest_device, new_local, centroids):
    n_group = lax.axis_size("group")
    n_member = lax.axis_size("member")
    devices = n_group * n_member
    row_dev, width = rows.shape
    lists = centroids.shape[0]
    capacity = max(2, 2 * row_dev // devices)
    group = lax.axis_index("group")
    core = lax.axis_index("member") & 1

    seen = [centroids]
    for shift in range(1, n_group):
        seen.append(lax.ppermute(centroids, "group", [(i, (i + shift) % n_group) for i in range(n_group)]))
    spare = -(n_group * lists) % SUB
    seen = jnp.concatenate(seen + [jnp.zeros((spare, width), f32)] * (spare > 0), axis=0)

    chunk = capacity // 2 if capacity % (2 * SUB) == 0 else capacity
    *outgoing, vectors, info, code = route(
        jnp.stack([group, core]),
        rows,
        old_list.reshape(1, -1),
        dest_device.reshape(1, -1),
        new_local.reshape(1, -1),
        old_centroids,
        (n_group, n_member, capacity, chunk),
    )
    outgoing = [x.reshape(devices, chunk, width) for x in outgoing]

    first = to_owners(outgoing[0])
    away = gram(vectors, code, seen, n_group, 1)
    kept = gram(vectors, code, seen, n_group, 0)
    parts = [(k, flip(x, "member", 0)) for k, x in zip(kept, away)]
    info, first = lax.optimization_barrier((info.reshape(devices, 1, BL), first))
    info = to_owners(info)[:, 0]
    pa, pb = sum_and_share(parts, n_group, n_member)
    counts = jnp.sum(info[:, capacity : capacity + lists], axis=0).astype(f32)
    count = lax.dynamic_index_in_dim(counts, core, 0, keepdims=True)
    scale = 1.0 / jnp.maximum(count, 1.0)
    arrived = [first]
    for later in outgoing[1:]:
        later, scale, pa, pb = lax.optimization_barrier((later, scale, pa, pb))
        arrived.append(to_owners(later))
    own = chol(pa, pb, scale, width)
    other = flip(own, "member", 0)
    own_inv = invert(own, width)
    other_inv = flip(own_inv, "member", 0)
    result, factors = whiten(arrived, info, own, other, own_inv, other_inv, core.reshape(1), centroids)
    return (result.reshape(devices * capacity, width), factors)


def solution(mesh):
    return jax.shard_map(
        on_device,
        mesh=mesh,
        in_specs=(
            P(("group", "member"), None),
            P(("group", "member")),
            P(),
            P(("group", "member"), None),
            P(("group", "member")),
            P("group", None),
        ),
        out_specs=(P(("group", "member"), None), P("group", None, None)),
        check_vma=False,
    )
```
